32 devices in a mesh: groups: 2 (over y), seq: 8 (over z, x), head: 2 (over core).
Axes of the slice: x: 2, y: 2, z: 4, core: 2. Of those that a mesh axis runs over, the one named last changes fastest.
Arguments:
- big_queries: bfloat16 [512, 4096], P(('groups', 'seq'), 'head'), parts along dimension 0, may hold values from -160 to 160
- big_keys: bfloat16 [512, 4096], P(('groups', 'seq'), 'head'), parts along dimension 0, may hold values from -8 to 8
- big_values: bfloat16 [512, 4096], P(('groups', 'seq'), 'head'), parts along dimension 0, may hold values from -6 to 6
- small_queries: bfloat16 [512, 1024], P(('groups', 'seq', 'head')), parts along dimension 0, may hold values from -160 to 160
- small_keys: bfloat16 [512, 1024], P(('groups', 'seq', 'head')), parts along dimension 0, may hold values from -8 to 8
- small_values: bfloat16 [512, 1024], P(('groups', 'seq', 'head')), parts along dimension 0, may hold values from -6 to 6
- big_readout: bfloat16 [4096, 64], P('head'), may hold values from -0.75 to 0.75
- small_readout: bfloat16 [1024, 64], replicated, may hold values from -1.5 to 1.5
- guidance: float32 [2], P('groups'), parts along dimension 0, may hold values from 1 to 4
Outputs:
- guided: float32 [256, 128], P(('groups', 'seq')), parts along dimension 0
The draws below stay inside these ranges and needn't reach their ends.
There are 2 independent parts, one for each index of `groups`. The reference program is written for one: setup_inputs(seed, part) draws one part's arguments, and reference() takes and returns one part's arrays. A program takes and returns all parts, laid end to end along the dimension named above; an argument that names none is the same for every part. Nothing has to cross between parts.
All inputs are finite; a program needn't handle non-finite values.
Results may differ from the reference program's by a relative error of at most 0.0035.
Values may be sent and summed in bfloat16 or wider, within the bound.
A program may use at most 64 MiB of HBM per device.

```python
import math
import jax
import jax.numpy as jnp
from jax import lax

DH = 128
HB = 32
HS = 8
LAT = 64
TOKENS = 256


def paired(key, heads, salt):
    folded = jax.random.fold_in(key, salt)
    query_seed, key_seed = jax.random.split(folded, 2)
    extent = (TOKENS, heads, DH)
    query_draw = jnp.clip(1.41 * jax.random.normal(query_seed, extent, jnp.float32), -8.0, 8.0)
    key_draw = jnp.clip(1.41 * jax.random.normal(key_seed, extent, jnp.float32), -8.0, 8.0)
    return (query_draw.reshape(TOKENS, heads * DH), key_draw.reshape(TOKENS, heads * DH))


def draw_big_queries(key, part):
    return paired(key, HB, 101)[0].astype(jnp.bfloat16)


def draw_big_keys(key, part):
    return paired(key, HB, 101)[1].astype(jnp.bfloat16)


def draw_small_queries(key, part):
    return paired(key, HS, 202)[0].astype(jnp.bfloat16)


def draw_small_keys(key, part):
    return paired(key, HS, 202)[1].astype(jnp.bfloat16)


def shard_levels(key, shape, cuts, least, top_value):
    def one(dim, shards_of):
        draws = jax.random.uniform(jax.random.fold_in(jax.random.fold_in(key, 6), dim), (shards_of,), jnp.float32, least / len(cuts), top_value / len(cuts))
        return jnp.repeat(jnp.exp(draws), shape[dim] // shards_of).reshape((-1,) + (1,) * (len(shape) - dim - 1))

    factor_of = one(*cuts[0])
    for cut in cuts[1:]:
        factor_of = factor_of * one(*cut)
    return factor_of


def gaussian(stream_key, dims, scale, limit, pieces=(), held_as=jnp.bfloat16):
    array = scale * jax.random.normal(stream_key, dims, jnp.float32)
    if pieces:
        array = array * shard_levels(stream_key, dims, pieces, -0.22, 0.18)
    return jnp.clip(array, -limit, limit).astype(held_as)


def setup_inputs(seed: int = 0, part: int = 0) -> dict:
    splits = jax.random.split(jax.random.key(seed), 10)
    part_keys = jax.random.split(jax.random.fold_in(splits[9], part), 10)
    big_queries = draw_big_queries(jax.random.fold_in(jax.random.fold_in(splits[9], part), 71), part)
    big_keys = draw_big_keys(jax.random.fold_in(jax.random.fold_in(splits[9], part), 71), part)
    big_values = gaussian(part_keys[2], (TOKENS, HB * DH), 1.0, 6.0, ((0, 8), (1, 2)))
    small_queries = draw_small_queries(jax.random.fold_in(jax.random.fold_in(splits[9], part), 71), part)
    small_keys = draw_small_keys(jax.random.fold_in(jax.random.fold_in(splits[9], part), 71), part)
    small_values = gaussian(part_keys[5], (TOKENS, HS * DH), 1.0, 6.0, ((0, 16),))
    big_readout = gaussian(splits[6], (HB * DH, LAT), (max(HB * DH // 64, 1)) ** -0.5, 0.75, ((0, 2),))
    small_readout = gaussian(splits[7], (HS * DH, LAT), (max(HS * DH // 64, 1)) ** -0.5, 1.5)
    guidance = jnp.clip(jax.random.uniform(part_keys[8], (1,), jnp.float32, 1.0, 4.0), 1.0, 4.0)
    return dict(big_queries=big_queries, big_keys=big_keys, big_values=big_values, small_queries=small_queries, small_keys=small_keys, small_values=small_values, big_readout=big_readout, small_readout=small_readout, guidance=guidance)


def attend_head(operands):
    query_head, key_head, value_head = operands
    scores = jnp.dot(query_head, key_head.T, preferred_element_type=jnp.float32) * (1.0 / math.sqrt(DH))
    row_max = lax.optimization_barrier(jnp.max(scores, axis=1, keepdims=True))
    probs = jnp.exp(scores - row_max)
    totals = lax.optimization_barrier(jnp.sum(probs, axis=1, keepdims=True))
    weights = probs.astype(jnp.bfloat16)
    attended = jnp.dot(weights, value_head, preferred_element_type=jnp.float32) / totals
    return attended.astype(jnp.bfloat16)

def split_model(matrix, heads):
    return jnp.transpose(matrix.reshape(TOKENS, heads, DH), (1, 0, 2))

def run_model(query_all, key_all, value_all, heads):
    outputs = lax.map(attend_head, (split_model(query_all, heads), split_model(key_all, heads), split_model(value_all, heads)))
    return jnp.transpose(outputs, (1, 0, 2)).reshape(TOKENS, heads * DH)

def reference(big_queries, big_keys, big_values, small_queries, small_keys, small_values, big_readout, small_readout, guidance):
    big_attention = run_model(big_queries, big_keys, big_values, HB)
    small_attention = run_model(small_queries, small_keys, small_values, HS)
    big_latent = jnp.dot(big_attention, big_readout, preferred_element_type=jnp.float32)
    small_latent = jnp.dot(small_attention, small_readout, preferred_element_type=jnp.float32)
    blended = big_latent + guidance[0] * (big_latent - small_latent)
    return blended.reshape(TOKENS // 2, 2 * LAT)
```

```python
import functools
import math

import jax
import jax.numpy as jnp
from jax import lax
from jax.experimental import pallas as pl
from jax.experimental.pallas import tpu as pltpu
from jax.sharding import PartitionSpec as P

DH = 128


def split_heads(matrix, blocks, parts):
    rows_here, columns = matrix.shape
    shaped = matrix.reshape(blocks, rows_here // blocks, parts, columns // parts)
    shaped = jnp.transpose(shaped, (0, 2, 1, 3))
    return shaped.reshape(blocks * parts, rows_here // blocks, columns // parts)


def copy_heads(matrix, blocks, parts):
    rows_here, columns = matrix.shape
    shaped = jnp.transpose(matrix.reshape(rows_here, parts, columns // parts), (1, 0, 2))
    shaped = jnp.broadcast_to(shaped[None], (blocks, parts, rows_here, columns // parts))
    return shaped.reshape(blocks * parts, rows_here, columns // parts)


def join_heads(stacked, blocks, parts):
    pieces, rows_here, columns = stacked.shape
    shaped = stacked.reshape(blocks, parts, rows_here, columns)
    shaped = jnp.transpose(shaped, (0, 2, 1, 3))
    return shaped.reshape(blocks * rows_here, parts * columns)


def attend(query_rows, key_rows, value_rows):
    query_count = query_rows.shape[0]
    heads_here = query_rows.shape[1] // DH
    key_count = key_rows.shape[0]
    block_height = math.gcd(query_count, 256)
    block_count = query_count // block_height
    query_blocks = query_rows.reshape(block_count, block_height, heads_here, DH)
    key_split = key_rows.reshape(key_count, heads_here, DH)
    value_split = value_rows.reshape(key_count, heads_here, DH)
    score_scale = 1.0 / math.sqrt(DH)

    def one_block(query_block):
        scores = (
            jnp.einsum("qgd,kgd->gqk", query_block, key_split, preferred_element_type=jnp.float32)
            * score_scale
        )
        row_max = jnp.max(scores, axis=2, keepdims=True)
        probs = jnp.exp(scores - row_max)
        totals = jnp.sum(probs, axis=2, keepdims=True)
        weights = probs.astype(jnp.bfloat16)
        accumulated = jnp.einsum(
            "gqk,kgd->gqd", weights, value_split, preferred_element_type=jnp.float32
        )
        attended = accumulated / totals
        attended = jnp.transpose(attended, (1, 0, 2)).reshape(block_height, heads_here * DH)
        return attended.astype(jnp.bfloat16)

    outputs = lax.map(one_block, query_blocks)
    return outputs.reshape(query_count, heads_here * DH)


def exchanged(
    big_queries,
    big_keys,
    big_values,
    small_queries,
    small_keys,
    small_values,
    big_readout,
    small_readout,
    guidance,
):
    seq_count = lax.axis_size("seq")
    big_heads = big_queries.shape[1] // DH
    big_group = max(big_heads // seq_count, 1)
    big_blocks = max(seq_count // big_heads, 1)
    big_parts = big_heads // big_group
    query_rows = lax.all_to_all(
        split_heads(big_queries, big_blocks, big_parts),
        "seq",
        split_axis=0,
        concat_axis=1,
        tiled=True,
    )[0]
    key_copies, value_copies = (
        lax.all_to_all(
            copy_heads(big_keys, big_blocks, big_parts),
            "seq",
            split_axis=0,
            concat_axis=1,
            tiled=True,
        ),
        lax.all_to_all(
            copy_heads(big_values, big_blocks, big_parts),
            "seq",
            split_axis=0,
            concat_axis=1,
            tiled=True,
        ),
    )
    key_rows = key_copies[0]
    value_rows = value_copies[0]
    big_out = attend(query_rows, key_rows, value_rows)
    big_back = lax.all_to_all(big_out[None], "seq", split_axis=1, concat_axis=0, tiled=True)
    big_attention = join_heads(big_back, big_blocks, big_parts)
    big_partial = jnp.dot(big_attention, big_readout, preferred_element_type=jnp.float32)
    small_heads = small_queries.shape[1] // DH
    small_group = max(small_heads // seq_count, 1)
    small_blocks = max(seq_count // small_heads, 1)
    small_parts = small_heads // small_group
    small_query_rows = lax.all_to_all(
        split_heads(small_queries, small_blocks, small_parts),
        "seq",
        split_axis=0,
        concat_axis=1,
        tiled=True,
    )[0]
    key_copies, value_copies = (
        lax.all_to_all(
            copy_heads(small_keys, small_blocks, small_parts),
            "seq",
            split_axis=0,
            concat_axis=1,
            tiled=True,
        ),
        lax.all_to_all(
            copy_heads(small_values, small_blocks, small_parts),
            "seq",
            split_axis=0,
            concat_axis=1,
            tiled=True,
        ),
    )
    small_key_rows, small_value_rows = (
        lax.all_gather(key_copies[0], "head", axis=0, tiled=True),
        lax.all_gather(value_copies[0], "head", axis=0, tiled=True),
    )
    small_out = attend(small_query_rows, small_key_rows, small_value_rows)
    small_back = lax.all_to_all(small_out[None], "seq", split_axis=1, concat_axis=0, tiled=True)
    small_attention = join_heads(small_back, small_blocks, small_parts)
    small_latent = jnp.dot(small_attention, small_readout, preferred_element_type=jnp.float32)
    weight_value = guidance[0]
    core_index = lax.axis_index("head")
    placed = lax.dynamic_update_slice(
        jnp.zeros_like(big_partial),
        small_latent,
        (core_index * small_latent.shape[0], jnp.zeros((), jnp.int32)),
    )
    blended = lax.psum((1.0 + weight_value) * big_partial - weight_value * placed, "head")
    return blended.reshape(blended.shape[0] // 2, 2 * blended.shape[1])


MESH = pl.DeviceIdType.MESH


def softmax_parts(query_head, key_head):
    scores = lax.dot_general(
        query_head, key_head, (((1,), (1,)), ((), ())), preferred_element_type=jnp.float32
    ) * (1.0 / math.sqrt(DH))
    row_max = jnp.max(scores, axis=1, keepdims=True)
    probs = jnp.exp(scores - row_max)
    totals = jnp.sum(probs, axis=1, keepdims=True)
    return probs.astype(jnp.bfloat16), totals


def read_out(values, readout):
    return lax.dot_general(
        values, readout, (((1,), (1,)), ((), ())), preferred_element_type=jnp.float32
    )


def window_kernel(
    n,
    m,
    guidance,
    big_q,
    big_k,
    big_v,
    small_q,
    small_k,
    small_v,
    big_read,
    small_read,
    out,
    all_q,
    all_k,
    all_w,
    few_q,
    few_k,
    few_w,
    own_v,
    own_few_v,
    read_big,
    read_small,
    ready_w,
    half_w,
    other_w,
    ready_few,
    weights,
    small_part,
    latent,
    stage,
    arrived,
    swap,
    guide,
    near,
    own_sem,
    big_send,
    big_recv,
    small_send,
    small_recv,
    few_send,
    few_recv,
    core_sem,
    back_send,
    back_recv,
    swap_sem,
):
    group = lax.axis_index("groups")
    me = lax.axis_index("seq")
    core = lax.axis_index("head")
    rungs = n // 2
    rung, side = lax.div(me, 2), lax.rem(me, 2)
    rows = big_q.shape[0]
    width = all_q.shape[1]
    few_rows = small_q.shape[0]
    few_width = few_q.shape[1]
    heads_here = width // DH
    lat = big_read.shape[0]
    half = rows // 2
    part = half // m

    def ahead(offset):
        return lax.rem(me + offset, n)

    def behind(offset):
        return lax.rem(me + n - offset, n)

    def offset_to(peer):
        return lax.rem(peer - me + n, n)

    def window(ref, index, size):
        return ref.at[:, pl.ds(pl.multiple_of(index * size, size), size)]

    def row_block(ref, index, size):
        return ref.at[pl.ds(pl.multiple_of(index * size, size), size), :]

    def toward(distance, act):
        for up in range(rungs - 1, -rungs, -1):
            across = distance - abs(up)
            if across not in (0, 1):
                continue
            peer = (rung + up) * 2 + lax.rem(side + across, 2)
            if up == 0:
                act(peer)
            elif up > 0:
                pl.when(rung + up < rungs)(functools.partial(act, peer))
            else:
                pl.when(rung + up >= 0)(functools.partial(act, peer))

    def key_rows(seq, which):
        return which * n + seq

    def query_rows(seq, which):
        return seq * m + which

    big_pairs = ((big_k, all_k), (big_q, all_q))
    few_pairs = ((small_k, few_k, key_rows), (small_q, few_q, query_rows))

    def big_copy(item, peer, offset):
        if item == 2:
            source, target = ready_w.at[peer], all_w
        else:
            source, target = window(big_pairs[item][0], peer, width), big_pairs[item][1]
        return pltpu.make_async_remote_copy(
            src_ref=source,
            dst_ref=row_block(target, me, rows),
            send_sem=big_send.at[item, offset],
            recv_sem=big_recv.at[item, offset],
            device_id=(group, peer, core),
            device_id_type=MESH,
        )

    def few_copy(item, peer, offset, which):
        source, target, place = few_pairs[item]
        return pltpu.make_async_remote_copy(
            src_ref=window(source, peer, few_width),
            dst_ref=row_block(target, place(me, which), few_rows),
            send_sem=small_send.at[item, offset],
            recv_sem=small_recv.at[item, offset, which],
            device_id=(group, peer, 0),
            device_id_type=MESH,
        )

    def few_w_copy(peer, offset):
        return pltpu.make_async_remote_copy(
            src_ref=ready_few.at[peer],
            dst_ref=row_block(few_w, me, few_rows),
            send_sem=few_send.at[offset],
            recv_sem=few_recv.at[offset],
            device_id=(group, peer, 0),
            device_id_type=MESH,
        )

    def core_copy():
        return pltpu.make_async_remote_copy(
            src_ref=half_w,
            dst_ref=other_w,
            send_sem=core_sem.at[0],
            recv_sem=core_sem.at[1],
            device_id=(group, me, 0),
            device_id_type=MESH,
        )

    def back_copy(peer, offset, turn, slot_core):
        target_core = lax.rem(core + turn, m)
        return pltpu.make_async_remote_copy(
            src_ref=stage.at[peer, target_core],
            dst_ref=arrived.at[offset, slot_core],
            send_sem=back_send.at[offset, turn],
            recv_sem=back_recv.at[offset, slot_core],
            device_id=(group, peer, target_core),
            device_id_type=MESH,
        )

    def swap_copy():
        return pltpu.make_async_remote_copy(
            src_ref=swap.at[0],
            dst_ref=swap.at[1],
            send_sem=swap_sem.at[0],
            recv_sem=swap_sem.at[1],
            device_id=(group, me, 1 - core),
            device_id_type=MESH,
        )

    barrier = pltpu.get_barrier_semaphore()
    neighbours = (
        1 + (rung > 0).astype(jnp.int32) + (rung < rungs - 1).astype(jnp.int32)
    )

    def greet(peer):
        for which in range(m):
            pl.semaphore_signal(
                barrier, inc=1, device_id=(group, peer, which), device_id_type=MESH
            )

    toward(1, greet)
    pl.semaphore_signal(
        barrier, inc=1, device_id=(group, me, 1 - core), device_id_type=MESH
    )

    value_copies = [
        pltpu.make_async_copy(big_v, own_v, own_sem.at[0]),
        pltpu.make_async_copy(big_read, read_big, own_sem.at[1]),
        pltpu.make_async_copy(small_v, own_few_v, own_sem.at[2]),
        pltpu.make_async_copy(small_read, read_small, own_sem.at[3]),
    ]
    own = [
        pltpu.make_async_copy(
            window(source, me, width), row_block(target, me, rows), own_sem.at[4 + item]
        )
        for item, (source, target) in enumerate(big_pairs)
    ]
    own.append(pltpu.make_async_copy(guidance, guide, own_sem.at[6]))
    few_own = [
        pltpu.make_async_copy(
            window(source, me, few_width),
            row_block(target, place(me, 0), few_rows),
            own_sem.at[7 + item],
        )
        for item, (source, target, place) in enumerate(few_pairs)
    ]
    for copy in value_copies + own:
        copy.start()

    @pl.when(core == 0)
    def _():
        for copy in few_own:
            copy.start()

    def start_scores(peer):
        offset = offset_to(peer)
        for item in (0, 1):
            few_copy(item, peer, offset, core).start()
        for item in (0, 1):
            big_copy(item, peer, offset).start()

    def pass_on(round_index):
        def act(peer):
            pl.semaphore_signal(
                near.at[round_index], inc=1, device_id=(group, peer, core), device_id_type=MESH
            )

        return act

    pl.semaphore_wait(barrier, m * neighbours + 1)
    toward(1, pass_on(0))
    toward(1, start_scores)

    @pl.when(core != 0)
    def _():
        for item in (0, 1):
            few_copy(item, me, 0, core).start()

    for copy in value_copies:
        copy.wait()
    few_lanes = lax.broadcasted_iota(jnp.int32, (few_rows, 2 * lat), 1)
    for seq in range(n):
        columns = slice(seq * few_width, (seq + 1) * few_width)
        term = read_out(own_few_v[:, columns], read_small[:, columns])
        both = jnp.concatenate([term, term], axis=1)
        mine = (few_lanes < lat) == (core == 0)
        half_w[seq] = jnp.where(mine, both, 0.0).astype(half_w.dtype)

    @pl.when(core != 0)
    def _():
        core_copy().start()

    for seq in range(n):
        terms = []
        for head in range(heads_here):
            columns = slice(seq * width + head * DH, seq * width + (head + 1) * DH)
            terms.append(read_out(own_v[:, columns], read_big[:, columns]))
        ready_w[seq] = jnp.concatenate(terms, axis=1).astype(ready_w.dtype)

    for distance in range(2, rungs + 1):
        pl.semaphore_wait(near.at[distance - 2], neighbours)
        if distance < rungs:
            toward(1, pass_on(distance - 1))
        toward(distance, start_scores)

    @pl.when(core == 0)
    def _():
        core_copy().wait_recv()
        ready_few[...] = half_w[...] + other_w[...]
        for distance in range(rungs, 0, -1):
            toward(distance, lambda peer: few_w_copy(peer, offset_to(peer)).start())
        few_w[pl.ds(pl.multiple_of(me * few_rows, few_rows), few_rows), :] = ready_few[me]

    for distance in range(rungs, 0, -1):
        toward(distance, lambda peer: big_copy(2, peer, offset_to(peer)).start())
    all_w[pl.ds(pl.multiple_of(me * rows, rows), rows), :] = ready_w[me]

    for copy in own:
        copy.wait()
    weight_value = guide[0]
    lanes = lax.broadcasted_iota(jnp.int32, latent.shape, 1)

    @pl.when(core == 0)
    def _():
        for copy in few_own:
            copy.wait()
        for offset in range(n):
            for which in range(m):
                if offset or which:
                    for item in (0, 1):
                        few_copy(item, behind(offset), offset, which).wait_recv()
        probs, totals = softmax_parts(few_q[...], few_k[...])
        for offset in range(1, n):
            few_w_copy(behind(offset), offset).wait_recv()
        keys = n * few_rows
        held = few_w[...]
        terms = [
            jnp.dot(
                probs[:, which * keys : (which + 1) * keys],
                held,
                preferred_element_type=jnp.float32,
            )
            for which in range(m)
        ]
        small_part[...] = weight_value * (jnp.where(lanes < lat, terms[0], terms[1]) / totals)

    @pl.when(core != 0)
    def _():
        small_part[...] = jnp.zeros_like(small_part)

    for offset in range(1, n):
        for item in (0, 1):
            big_copy(item, behind(offset), offset).wait_recv()
    totals_of = []
    for head in range(heads_here):
        columns = slice(head * DH, (head + 1) * DH)
        probs, totals = softmax_parts(all_q[:, columns], all_k[:, columns])
        weights[head] = probs
        totals_of.append(totals)
    for offset in range(1, n):
        big_copy(2, behind(offset), offset).wait_recv()
    held = all_w[...]
    terms = [
        jnp.dot(weights[head], held, preferred_element_type=jnp.float32) / totals_of[head]
        for head in range(heads_here)
    ]
    term = (1.0 + weight_value) * jnp.where(lanes < lat, terms[0], terms[1]) - small_part[...]
    latent[...] = term + pltpu.roll(term, lat, 1)
    pair_rows = latent.shape[0] // 2
    even = latent[pl.ds(0, pair_rows, stride=2), :]
    odd = latent[pl.ds(1, pair_rows, stride=2), :]
    paired = jnp.where(lanes[:pair_rows] < lat, even, odd)
    stage[...] = paired.reshape(n, m, part, 2 * lat)
    arrived[0, core] = stage[me, core]

    for distance in range(rungs, 0, -1):

        def start_back(peer):
            for turn in range(m):
                back_copy(peer, offset_to(peer), turn, core).start()

        toward(distance, start_back)
    for turn in range(1, m):
        back_copy(me, 0, turn, core).start()
    for turn in range(1, m):
        back_copy(me, 0, turn, lax.rem(core + turn, m)).wait_recv()
    for offset in range(1, n):
        for slot_core in range(m):
            back_copy(behind(offset), offset, 0, slot_core).wait_recv()
    swap[0] = jnp.sum(arrived[...].reshape(n * m, part, 2 * lat), axis=0)
    swap_copy().start()
    out[pl.ds(pl.multiple_of(core * part, part), part), :] = swap[0]

    for offset in range(1, n):
        for item in (0, 1):
            few_copy(item, ahead(offset), offset, core).wait_send()
        for item in range(3):
            big_copy(item, ahead(offset), offset).wait_send()
        for turn in range(m):
            back_copy(ahead(offset), offset, turn, core).wait_send()
    for turn in range(1, m):
        back_copy(me, 0, turn, core).wait_send()

    @pl.when(core == 0)
    def _():
        for offset in range(1, n):
            few_w_copy(ahead(offset), offset).wait_send()

    @pl.when(core != 0)
    def _():
        for item in (0, 1):
            few_copy(item, me, 0, core).wait_send()
        core_copy().wait_send()

    swap_copy().wait()
    out[pl.ds(pl.multiple_of((1 - core) * part, part), part), :] = swap[1]


def fused(
    n,
    m,
    big_queries,
    big_keys,
    big_values,
    small_queries,
    small_keys,
    small_values,
    big_readout,
    small_readout,
    guidance,
):
    rows, columns = big_queries.shape
    few_rows, few_columns = small_queries.shape
    width, few_width = columns // n, few_columns // n
    tokens = rows * n
    lat = big_readout.shape[1]
    half = rows // 2
    part = half // m
    kind = jnp.bfloat16
    dma = pltpu.SemaphoreType.DMA
    return pl.pallas_call(
        functools.partial(window_kernel, n, m),
        out_shape=pltpu.VMEM((half, 2 * lat), jnp.float32),
        in_specs=[pl.BlockSpec(memory_space=pl.ANY)] * 9,
        out_specs=pl.BlockSpec(memory_space=pltpu.VMEM),
        scratch_shapes=[
            pltpu.VMEM((tokens, width), kind),
            pltpu.VMEM((tokens, width), kind),
            pltpu.VMEM((tokens, 2 * lat), kind),
            pltpu.VMEM((tokens, few_width), kind),
            pltpu.VMEM((tokens, few_width), kind),
            pltpu.VMEM((n * few_rows, 2 * lat), kind),
            pltpu.VMEM((rows, columns), kind),
            pltpu.VMEM((few_rows, few_columns), kind),
            pltpu.VMEM((lat, columns), kind),
            pltpu.VMEM((lat, few_columns), kind),
            pltpu.VMEM((n, rows, 2 * lat), kind),
            pltpu.VMEM((n, few_rows, 2 * lat), kind),
            pltpu.VMEM((n, few_rows, 2 * lat), kind),
            pltpu.VMEM((n, few_rows, 2 * lat), kind),
            pltpu.VMEM((width // DH, tokens, tokens), kind),
            pltpu.VMEM((tokens, 2 * lat), jnp.float32),
            pltpu.VMEM((tokens, 2 * lat), jnp.float32),
            pltpu.VMEM((n, m, part, 2 * lat), jnp.float32),
            pltpu.VMEM((n, m, part, 2 * lat), jnp.float32),
            pltpu.VMEM((2, part, 2 * lat), jnp.float32),
            pltpu.SMEM((1,), jnp.float32),
            pltpu.SemaphoreType.REGULAR((n // 2 - 1,)),
            dma((9,)),
            dma((3, n)),
            dma((3, n)),
            dma((2, n)),
            dma((2, n, m)),
            dma((n,)),
            dma((n,)),
            dma((2,)),
            dma((n, m)),
            dma((n, m)),
            dma((2,)),
        ],
        compiler_params=pltpu.CompilerParams(collective_id=0, has_side_effects=True),
        name="fused_window",
    )(
        guidance,
        big_queries,
        big_keys,
        big_values,
        small_queries,
        small_keys,
        small_values,
        big_readout.T,
        small_readout.T,
    )


def fits(n, m, big_queries, small_queries, lat):
    rows, columns = big_queries.shape
    few_rows, few_columns = small_queries.shape
    return (
        n > 2
        and n % 2 == 0
        and m == 2
        and n * rows <= 512
        and columns == 2 * n * DH
        and few_columns == n * DH
        and rows == m * few_rows
        and few_rows % 16 == 0
        and 2 * lat == 128
    )


def shards(*arguments):
    n, m = lax.axis_size("seq"), lax.axis_size("head")
    if fits(n, m, arguments[0], arguments[3], arguments[6].shape[1]):
        return fused(n, m, *arguments)
    return exchanged(*arguments)


def solution(mesh):
    placed = (
        P(("groups", "seq"), "head"),
        P(("groups", "seq"), "head"),
        P(("groups", "seq"), "head"),
        P(("groups", "seq", "head"), None),
        P(("groups", "seq", "head"), None),
        P(("groups", "seq", "head"), None),
        P("head", None),
        P(),
        P("groups"),
    )
    return jax.shard_map(
        shards, mesh=mesh, in_specs=placed, out_specs=P(("groups", "seq"), None), check_vma=False
    )
```

```python
import functools
import math

import jax
import jax.numpy as jnp
from jax import lax
from jax.experimental import pallas as pl
from jax.experimental.pallas import tpu as pltpu
from jax.sharding import PartitionSpec as P

DH = 128


def split_heads(matrix, blocks, parts):
    rows_here, columns = matrix.shape
    shaped = matrix.reshape(blocks, rows_here // blocks, parts, columns // parts)
    shaped = jnp.transpose(shaped, (0, 2, 1, 3))
    return shaped.reshape(blocks * parts, rows_here // blocks, columns // parts)


def copy_heads(matrix, blocks, parts):
    rows_here, columns = matrix.shape
    shaped = jnp.transpose(matrix.reshape(rows_here, parts, columns // parts), (1, 0, 2))
    shaped = jnp.broadcast_to(shaped[None], (blocks, parts, rows_here, columns // parts))
    return shaped.reshape(blocks * parts, rows_here, columns // parts)


def join_heads(stacked, blocks, parts):
    pieces, rows_here, columns = stacked.shape
    shaped = stacked.reshape(blocks, parts, rows_here, columns)
    shaped = jnp.transpose(shaped, (0, 2, 1, 3))
    return shaped.reshape(blocks * rows_here, parts * columns)


def attend(query_rows, key_rows, value_rows):
    query_count = query_rows.shape[0]
    heads_here = query_rows.shape[1] // DH
    key_count = key_rows.shape[0]
    block_height = math.gcd(query_count, 256)
    block_count = query_count // block_height
    query_blocks = query_rows.reshape(block_count, block_height, heads_here, DH)
    key_split = key_rows.reshape(key_count, heads_here, DH)
    value_split = value_rows.reshape(key_count, heads_here, DH)
    score_scale = 1.0 / math.sqrt(DH)

    def one_block(query_block):
        scores = (
            jnp.einsum("qgd,kgd->gqk", query_block, key_split, preferred_element_type=jnp.float32)
            * score_scale
        )
        row_max = jnp.max(scores, axis=2, keepdims=True)
        probs = jnp.exp(scores - row_max)
        totals = jnp.sum(probs, axis=2, keepdims=True)
        weights = probs.astype(jnp.bfloat16)
        accumulated = jnp.einsum(
            "gqk,kgd->gqd", weights, value_split, preferred_element_type=jnp.float32
        )
        attended = accumulated / totals
        attended = jnp.transpose(attended, (1, 0, 2)).reshape(block_height, heads_here * DH)
        return attended.astype(jnp.bfloat16)

    outputs = lax.map(one_block, query_blocks)
    return outputs.reshape(query_count, heads_here * DH)


def exchanged(
    big_queries,
    big_keys,
    big_values,
    small_queries,
    small_keys,
    small_values,
    big_readout,
    small_readout,
    guidance,
):
    seq_count = lax.axis_size("seq")
    big_heads = big_queries.shape[1] // DH
    big_group = max(big_heads // seq_count, 1)
    big_blocks = max(seq_count // big_heads, 1)
    big_parts = big_heads // big_group
    query_rows = lax.all_to_all(
        split_heads(big_queries, big_blocks, big_parts),
        "seq",
        split_axis=0,
        concat_axis=1,
        tiled=True,
    )[0]
    key_copies, value_copies = (
        lax.all_to_all(
            copy_heads(big_keys, big_blocks, big_parts),
            "seq",
            split_axis=0,
            concat_axis=1,
            tiled=True,
        ),
        lax.all_to_all(
            copy_heads(big_values, big_blocks, big_parts),
            "seq",
            split_axis=0,
            concat_axis=1,
            tiled=True,
        ),
    )
    key_rows = key_copies[0]
    value_rows = value_copies[0]
    big_out = attend(query_rows, key_rows, value_rows)
    big_back = lax.all_to_all(big_out[None], "seq", split_axis=1, concat_axis=0, tiled=True)
    big_attention = join_heads(big_back, big_blocks, big_parts)
    big_partial = jnp.dot(big_attention, big_readout, preferred_element_type=jnp.float32)
    small_heads = small_queries.shape[1] // DH
    small_group = max(small_heads // seq_count, 1)
    small_blocks = max(seq_count // small_heads, 1)
    small_parts = small_heads // small_group
    small_query_rows = lax.all_to_all(
        split_heads(small_queries, small_blocks, small_parts),
        "seq",
        split_axis=0,
        concat_axis=1,
        tiled=True,
    )[0]
    key_copies, value_copies = (
        lax.all_to_all(
            copy_heads(small_keys, small_blocks, small_parts),
            "seq",
            split_axis=0,
            concat_axis=1,
            tiled=True,
        ),
        lax.all_to_all(
            copy_heads(small_values, small_blocks, small_parts),
            "seq",
            split_axis=0,
            concat_axis=1,
            tiled=True,
        ),
    )
    small_key_rows, small_value_rows = (
        lax.all_gather(key_copies[0], "head", axis=0, tiled=True),
        lax.all_gather(value_copies[0], "head", axis=0, tiled=True),
    )
    small_out = attend(small_query_rows, small_key_rows, small_value_rows)
    small_back = lax.all_to_all(small_out[None], "seq", split_axis=1, concat_axis=0, tiled=True)
    small_attention = join_heads(small_back, small_blocks, small_parts)
    small_latent = jnp.dot(small_attention, small_readout, preferred_element_type=jnp.float32)
    weight_value = guidance[0]
    core_index = lax.axis_index("head")
    placed = lax.dynamic_update_slice(
        jnp.zeros_like(big_partial),
        small_latent,
        (core_index * small_latent.shape[0], jnp.zeros((), jnp.int32)),
    )
    blended = lax.psum((1.0 + weight_value) * big_partial - weight_value * placed, "head")
    return blended.reshape(blended.shape[0] // 2, 2 * blended.shape[1])


MESH = pl.DeviceIdType.MESH


def softmax_parts(query_head, key_head):
    scores = lax.dot_general(
        query_head, key_head, (((1,), (1,)), ((), ())), preferred_element_type=jnp.float32
    ) * (1.0 / math.sqrt(DH))
    row_max = jnp.max(scores, axis=1, keepdims=True)
    probs = jnp.exp(scores - row_max)
    totals = jnp.sum(probs, axis=1, keepdims=True)
    return probs.astype(jnp.bfloat16), totals


def read_out(values, readout):
    return lax.dot_general(
        values, readout, (((1,), (1,)), ((), ())), preferred_element_type=jnp.float32
    )


def window_kernel(
    n,
    m,
    guidance,
    big_q,
    big_k,
    big_v,
    small_q,
    small_k,
    small_v,
    big_read,
    small_read,
    out,
    all_q,
    all_k,
    all_w,
    few_q,
    few_k,
    few_v,
    own_v,
    read_big,
    read_small,
    ready_w,
    weights,
    small_part,
    latent,
    stage,
    arrived,
    swap,
    guide,
    near,
    own_sem,
    big_send,
    big_recv,
    value_sem,
    few_send,
    few_recv,
    back_sem,
    swap_sem,
):
    group = lax.axis_index("groups")
    me = lax.axis_index("seq")
    core = lax.axis_index("head")
    host = m - 1
    rungs = n // 2
    rung, side = lax.div(me, 2), lax.rem(me, 2)
    rows = big_q.shape[0]
    width = all_q.shape[1]
    few_rows = small_q.shape[0]
    few_width = few_q.shape[1]
    heads_here = width // DH
    lat = big_read.shape[0]
    half = rows // 2
    part = half // m

    def window(ref, index, size):
        return ref.at[:, pl.ds(pl.multiple_of(index * size, size), size)]

    def row_block(ref, index, size):
        return ref.at[pl.ds(pl.multiple_of(index * size, size), size), :]

    def toward(distance, act, crossing=None):
        for up in sorted(range(1 - rungs, rungs), key=lambda up: -abs(up)):
            if distance - abs(up) not in (0, 1):
                continue
            there = rung + up
            wanted = (there >= 0) & (there < rungs)
            if crossing is not None:
                other = (rung < rungs // 2) != (there < rungs // 2)
                wanted = wanted & (other if crossing else jnp.logical_not(other))
            peer = there * 2 + lax.rem(side + distance - abs(up), 2)
            pl.when(wanted)(functools.partial(act, peer))

    def chips_at(distance):
        count = 0
        for up in range(1 - rungs, rungs):
            if distance - abs(up) in (0, 1):
                there = rung + up
                count = count + ((there >= 0) & (there < rungs)).astype(jnp.int32)
        return count

    big_pairs = ((big_k, all_k), (big_q, all_q))
    few_pairs = ((small_k, few_k), (small_q, few_q), (small_v, few_v))

    def head_window(ref, seq, head):
        return ref.at[:, pl.ds(pl.multiple_of(seq * width + head * DH, DH), DH)]

    def head_rows(ref, seq, head):
        return ref.at[pl.ds(pl.multiple_of(seq * rows, rows), rows), pl.ds(head * DH, DH)]

    def big_copy(item, head, peer):
        source, target = big_pairs[item]
        return pltpu.make_async_remote_copy(
            src_ref=head_window(source, peer, head),
            dst_ref=head_rows(target, me, head),
            send_sem=big_send.at[item],
            recv_sem=big_recv.at[item, head],
            device_id=(group, peer, core),
            device_id_type=MESH,
        )

    def value_copy(peer):
        return pltpu.make_async_remote_copy(
            src_ref=ready_w.at[peer],
            dst_ref=row_block(all_w, me, rows),
            send_sem=value_sem.at[0],
            recv_sem=value_sem.at[1],
            device_id=(group, peer, core),
            device_id_type=MESH,
        )

    def few_copy(item, peer):
        source, target = few_pairs[item]
        return pltpu.make_async_remote_copy(
            src_ref=window(source, peer, few_width),
            dst_ref=row_block(target, me * m + core, few_rows),
            send_sem=few_send.at[item],
            recv_sem=few_recv.at[item],
            device_id=(group, peer, host),
            device_id_type=MESH,
        )

    def back_copy(peer, which):
        return pltpu.make_async_remote_copy(
            src_ref=stage.at[peer * m + which],
            dst_ref=arrived.at[me * m + core],
            send_sem=back_sem.at[0],
            recv_sem=back_sem.at[1],
            device_id=(group, peer, which),
            device_id_type=MESH,
        )

    def swap_copy():
        return pltpu.make_async_remote_copy(
            src_ref=swap.at[0],
            dst_ref=swap.at[1],
            send_sem=swap_sem.at[0],
            recv_sem=swap_sem.at[1],
            device_id=(group, me, 1 - core),
            device_id_type=MESH,
        )

    def await_bytes(ref, sem):
        pltpu.make_async_copy(ref, ref, sem).wait()

    barrier = pltpu.get_barrier_semaphore()

    def greet(peer):
        for which in range(m):
            pl.semaphore_signal(
                barrier, inc=1, device_id=(group, peer, which), device_id_type=MESH
            )

    toward(1, greet)
    pl.semaphore_signal(
        barrier, inc=1, device_id=(group, me, 1 - core), device_id_type=MESH
    )

    value_copies = [
        pltpu.make_async_copy(big_v, own_v, own_sem.at[0]),
        pltpu.make_async_copy(big_read, read_big, own_sem.at[1]),
    ]
    for copy in value_copies:
        copy.start()
    late_copies = [
        pltpu.make_async_copy(guidance, guide, own_sem.at[2]),
        pltpu.make_async_copy(window(small_read, me, few_width), read_small, own_sem.at[3]),
    ]
    for copy in late_copies:
        copy.start()
    for head in range(heads_here):
        for item, (source, target) in enumerate(big_pairs):
            pltpu.make_async_copy(
                head_window(source, me, head),
                head_rows(target, me, head),
                big_recv.at[item, head],
            ).start()

    @pl.when(core == host)
    def _():
        for item in range(3):
            source, target = few_pairs[item]
            pltpu.make_async_copy(
                window(source, me, few_width),
                row_block(target, me * m + host, few_rows),
                few_recv.at[item],
            ).start()

    for copy in value_copies:
        copy.wait()
    for seq in range(n):
        terms = []
        for head in range(heads_here):
            columns = slice(seq * width + head * DH, seq * width + (head + 1) * DH)
            terms.append(read_out(own_v[:, columns], read_big[:, columns]))
        ready_w[seq] = jnp.concatenate(terms, axis=1).astype(ready_w.dtype)

    def start_few(peer):
        for item in range(3):
            few_copy(item, peer).start()

    def start_head(head, peer):
        for item in (0, 1):
            big_copy(item, head, peer).start()

    def start_early(peer):
        start_few(peer)
        start_head(0, peer)
        value_copy(peer).start()

    def start_late(peer):
        for head in range(1, heads_here):
            start_head(head, peer)

    def pass_on(index):
        def act(peer):
            pl.semaphore_signal(
                near.at[index], inc=1, device_id=(group, peer, core), device_id_type=MESH
            )

        return act

    pl.semaphore_wait(barrier, m * chips_at(1) + m - 1)
    toward(1, pass_on(0))
    toward(1, start_early, True)
    toward(1, start_late, True)
    toward(1, start_early, False)
    known, index = 1, 0
    while known < rungs:
        pl.semaphore_wait(near.at[index], chips_at(known))
        reach = min(2 * known, rungs)
        index += 1
        if reach < rungs:
            toward(reach, pass_on(index))
        for distance in range(known + 1, reach + 1):
            toward(distance, start_early, True)
            toward(distance, start_early, False)
        held, known = known, reach
    for distance in range(held + 1, rungs + 1):
        toward(distance, start_late)
    for distance in range(held, 1, -1):
        toward(distance, start_late)
    toward(1, start_late, False)

    @pl.when(core != host)
    def _():
        for item in range(3):
            few_copy(item, me).start()

    all_w[pl.ds(pl.multiple_of(me * rows, rows), rows), :] = ready_w[me]
    for copy in late_copies:
        copy.wait()
    weight_value = guide[0]
    lanes = lax.broadcasted_iota(jnp.int32, latent.shape, 1)

    @pl.when(core == host)
    def _():
        for item in range(3):
            await_bytes(few_pairs[item][1], few_recv.at[item])
        probs, totals = softmax_parts(few_q[...], few_k[...])
        attended = jnp.dot(probs, few_v[...], preferred_element_type=jnp.float32) / totals
        term = read_out(attended.astype(few_v.dtype), read_small[...])
        small_part[...] = weight_value * jnp.concatenate([term, jnp.zeros_like(term)], axis=1)

    @pl.when(core != host)
    def _():
        small_part[...] = jnp.zeros_like(small_part)

    for head in range(heads_here):
        columns = slice(head * DH, (head + 1) * DH)
        for item, (source, target) in enumerate(big_pairs):
            await_bytes(target.at[:, columns], big_recv.at[item, head])
        probs, totals = softmax_parts(all_q[:, columns], all_k[:, columns])
        if head == 0:
            weights[...] = probs
            await_bytes(all_w.at[pl.ds(0, (n - 1) * rows), :], value_sem.at[1])
            probs = weights[...]
        term = jnp.dot(probs, all_w[...], preferred_element_type=jnp.float32) / totals
        term = (1.0 + weight_value) * term
        if head == 0:
            small_part[...] = term - small_part[...]
    term = jnp.where(lanes < lat, small_part[...], term)
    latent[...] = term + pltpu.roll(term, lat, 1)
    pair_rows = latent.shape[0] // 2
    even = latent[pl.ds(0, pair_rows, stride=2), :]
    odd = latent[pl.ds(1, pair_rows, stride=2), :]
    paired = jnp.where(lanes[:pair_rows] < lat, even, odd)
    stage[...] = paired.reshape(n * m, part, 2 * lat)
    arrived[me * m + core] = stage[me * m + core]

    def start_back(peer):
        for which in range(m):
            back_copy(peer, which).start()

    for distance in range(rungs, 0, -1):
        toward(distance, start_back)
    back_copy(me, 1 - core).start()
    everyone = arrived.at[pl.ds(0, n * m - 1)]
    await_bytes(everyone, back_sem.at[1])
    swap[0] = jnp.sum(arrived[...], axis=0)
    swap_copy().start()
    out[pl.ds(pl.multiple_of(core * part, part), part), :] = swap[0]

    for item in (0, 1):
        await_bytes(big_pairs[item][1].at[pl.ds(0, (n - 1) * rows), :], big_send.at[item])
    await_bytes(all_w.at[pl.ds(0, (n - 1) * rows), :], value_sem.at[0])
    await_bytes(everyone, back_sem.at[0])

    @pl.when(core == host)
    def _():
        for item in range(3):
            await_bytes(few_pairs[item][1].at[pl.ds(0, (n - 1) * few_rows), :], few_send.at[item])

    @pl.when(core != host)
    def _():
        for item in range(3):
            await_bytes(few_pairs[item][1].at[pl.ds(0, n * few_rows), :], few_send.at[item])

    swap_copy().wait()
    out[pl.ds(pl.multiple_of((1 - core) * part, part), part), :] = swap[1]


def fused(
    n,
    m,
    big_queries,
    big_keys,
    big_values,
    small_queries,
    small_keys,
    small_values,
    big_readout,
    small_readout,
    guidance,
):
    rows, columns = big_queries.shape
    few_rows, few_columns = small_queries.shape
    width, few_width = columns // n, few_columns // n
    tokens = rows * n
    lat = big_readout.shape[1]
    half = rows // 2
    part = half // m
    kind = jnp.bfloat16
    dma = pltpu.SemaphoreType.DMA
    return pl.pallas_call(
        functools.partial(window_kernel, n, m),
        out_shape=pltpu.VMEM((half, 2 * lat), jnp.float32),
        in_specs=[pl.BlockSpec(memory_space=pl.ANY)] * 9,
        out_specs=pl.BlockSpec(memory_space=pltpu.VMEM),
        scratch_shapes=[
            pltpu.VMEM((tokens, width), kind),
            pltpu.VMEM((tokens, width), kind),
            pltpu.VMEM((tokens, 2 * lat), kind),
            pltpu.VMEM((tokens, few_width), kind),
            pltpu.VMEM((tokens, few_width), kind),
            pltpu.VMEM((tokens, few_width), kind),
            pltpu.VMEM((rows, columns), kind),
            pltpu.VMEM((lat, columns), kind),
            pltpu.VMEM((lat, few_width), kind),
            pltpu.VMEM((n, rows, 2 * lat), kind),
            pltpu.VMEM((tokens, tokens), kind),
            pltpu.VMEM((tokens, 2 * lat), jnp.float32),
            pltpu.VMEM((tokens, 2 * lat), jnp.float32),
            pltpu.VMEM((n * m, part, 2 * lat), jnp.float32),
            pltpu.VMEM((n * m, part, 2 * lat), jnp.float32),
            pltpu.VMEM((2, part, 2 * lat), jnp.float32),
            pltpu.SMEM((1,), jnp.float32),
            pltpu.SemaphoreType.REGULAR(((n // 2 - 1).bit_length(),)),
            dma((4,)),
            dma((2,)),
            dma((2, width // DH)),
            dma((2,)),
            dma((3,)),
            dma((3,)),
            dma((2,)),
            dma((2,)),
        ],
        compiler_params=pltpu.CompilerParams(collective_id=0, has_side_effects=True),
        name="fused_window",
    )(
        guidance,
        big_queries,
        big_keys,
        big_values,
        small_queries,
        small_keys,
        small_values,
        big_readout.T,
        small_readout.T,
    )


def fits(n, m, big_queries, small_queries, lat):
    rows, columns = big_queries.shape
    few_rows, few_columns = small_queries.shape
    return (
        n > 2
        and n % 2 == 0
        and m == 2
        and n * rows <= 512
        and columns == 2 * n * DH
        and few_columns == n * DH
        and rows == m * few_rows
        and few_rows % 16 == 0
        and 2 * lat == 128
    )


def shards(*arguments):
    n, m = lax.axis_size("seq"), lax.axis_size("head")
    if fits(n, m, arguments[0], arguments[3], arguments[6].shape[1]):
        return fused(n, m, *arguments)
    return exchanged(*arguments)


def solution(mesh):
    placed = (
        P(("groups", "seq"), "head"),
        P(("groups", "seq"), "head"),
        P(("groups", "seq"), "head"),
        P(("groups", "seq", "head"), None),
        P(("groups", "seq", "head"), None),
        P(("groups", "seq", "head"), None),
        P("head", None),
        P(),
        P("groups"),
    )
    return jax.shard_map(
        shards, mesh=mesh, in_specs=placed, out_specs=P(("groups", "seq"), None), check_vma=False
    )
```

```python
import functools
import math

import jax
import jax.numpy as jnp
from jax import lax
from jax.experimental import pallas as pl
from jax.experimental.pallas import tpu as pltpu
from jax.sharding import PartitionSpec as P

DH = 128


def split_heads(matrix, blocks, parts):
    rows_here, columns = matrix.shape
    shaped = matrix.reshape(blocks, rows_here // blocks, parts, columns // parts)
    shaped = jnp.transpose(shaped, (0, 2, 1, 3))
    return shaped.reshape(blocks * parts, rows_here // blocks, columns // parts)


def copy_heads(matrix, blocks, parts):
    rows_here, columns = matrix.shape
    shaped = jnp.transpose(matrix.reshape(rows_here, parts, columns // parts), (1, 0, 2))
    shaped = jnp.broadcast_to(shaped[None], (blocks, parts, rows_here, columns // parts))
    return shaped.reshape(blocks * parts, rows_here, columns // parts)


def join_heads(stacked, blocks, parts):
    pieces, rows_here, columns = stacked.shape
    shaped = stacked.reshape(blocks, parts, rows_here, columns)
    shaped = jnp.transpose(shaped, (0, 2, 1, 3))
    return shaped.reshape(blocks * rows_here, parts * columns)


def attend(query_rows, key_rows, value_rows):
    query_count = query_rows.shape[0]
    heads_here = query_rows.shape[1] // DH
    key_count = key_rows.shape[0]
    block_height = math.gcd(query_count, 256)
    block_count = query_count // block_height
    query_blocks = query_rows.reshape(block_count, block_height, heads_here, DH)
    key_split = key_rows.reshape(key_count, heads_here, DH)
    value_split = value_rows.reshape(key_count, heads_here, DH)
    score_scale = 1.0 / math.sqrt(DH)

    def one_block(query_block):
        scores = (
            jnp.einsum("qgd,kgd->gqk", query_block, key_split, preferred_element_type=jnp.float32)
            * score_scale
        )
        row_max = jnp.max(scores, axis=2, keepdims=True)
        probs = jnp.exp(scores - row_max)
        totals = jnp.sum(probs, axis=2, keepdims=True)
        weights = probs.astype(jnp.bfloat16)
        accumulated = jnp.einsum(
            "gqk,kgd->gqd", weights, value_split, preferred_element_type=jnp.float32
        )
        attended = accumulated / totals
        attended = jnp.transpose(attended, (1, 0, 2)).reshape(block_height, heads_here * DH)
        return attended.astype(jnp.bfloat16)

    outputs = lax.map(one_block, query_blocks)
    return outputs.reshape(query_count, heads_here * DH)


def exchanged(
    big_queries,
    big_keys,
    big_values,
    small_queries,
    small_keys,
    small_values,
    big_readout,
    small_readout,
    guidance,
):
    seq_count = lax.axis_size("seq")
    big_heads = big_queries.shape[1] // DH
    big_group = max(big_heads // seq_count, 1)
    big_blocks = max(seq_count // big_heads, 1)
    big_parts = big_heads // big_group
    query_rows = lax.all_to_all(
        split_heads(big_queries, big_blocks, big_parts),
        "seq",
        split_axis=0,
        concat_axis=1,
        tiled=True,
    )[0]
    key_copies, value_copies = (
        lax.all_to_all(
            copy_heads(big_keys, big_blocks, big_parts),
            "seq",
            split_axis=0,
            concat_axis=1,
            tiled=True,
        ),
        lax.all_to_all(
            copy_heads(big_values, big_blocks, big_parts),
            "seq",
            split_axis=0,
            concat_axis=1,
            tiled=True,
        ),
    )
    key_rows = key_copies[0]
    value_rows = value_copies[0]
    big_out = attend(query_rows, key_rows, value_rows)
    big_back = lax.all_to_all(big_out[None], "seq", split_axis=1, concat_axis=0, tiled=True)
    big_attention = join_heads(big_back, big_blocks, big_parts)
    big_partial = jnp.dot(big_attention, big_readout, preferred_element_type=jnp.float32)
    small_heads = small_queries.shape[1] // DH
    small_group = max(small_heads // seq_count, 1)
    small_blocks = max(seq_count // small_heads, 1)
    small_parts = small_heads // small_group
    small_query_rows = lax.all_to_all(
        split_heads(small_queries, small_blocks, small_parts),
        "seq",
        split_axis=0,
        concat_axis=1,
        tiled=True,
    )[0]
    key_copies, value_copies = (
        lax.all_to_all(
            copy_heads(small_keys, small_blocks, small_parts),
            "seq",
            split_axis=0,
            concat_axis=1,
            tiled=True,
        ),
        lax.all_to_all(
            copy_heads(small_values, small_blocks, small_parts),
            "seq",
            split_axis=0,
            concat_axis=1,
            tiled=True,
        ),
    )
    small_key_rows, small_value_rows = (
        lax.all_gather(key_copies[0], "head", axis=0, tiled=True),
        lax.all_gather(value_copies[0], "head", axis=0, tiled=True),
    )
    small_out = attend(small_query_rows, small_key_rows, small_value_rows)
    small_back = lax.all_to_all(small_out[None], "seq", split_axis=1, concat_axis=0, tiled=True)
    small_attention = join_heads(small_back, small_blocks, small_parts)
    small_latent = jnp.dot(small_attention, small_readout, preferred_element_type=jnp.float32)
    weight_value = guidance[0]
    core_index = lax.axis_index("head")
    placed = lax.dynamic_update_slice(
        jnp.zeros_like(big_partial),
        small_latent,
        (core_index * small_latent.shape[0], jnp.zeros((), jnp.int32)),
    )
    blended = lax.psum((1.0 + weight_value) * big_partial - weight_value * placed, "head")
    return blended.reshape(blended.shape[0] // 2, 2 * blended.shape[1])


MESH = pl.DeviceIdType.MESH


def softmax_parts(query_head, key_head):
    scores = lax.dot_general(
        query_head, key_head, (((1,), (1,)), ((), ())), preferred_element_type=jnp.float32
    ) * (1.0 / math.sqrt(DH))
    row_max = jnp.max(scores, axis=1, keepdims=True)
    probs = jnp.exp(scores - row_max)
    totals = jnp.sum(probs, axis=1, keepdims=True)
    return probs.astype(jnp.bfloat16), totals


def read_out(values, readout):
    return lax.dot_general(
        values, readout, (((1,), (1,)), ((), ())), preferred_element_type=jnp.float32
    )


def window_kernel(
    n,
    m,
    guidance,
    big_q,
    big_k,
    big_v,
    small_q,
    small_k,
    small_v,
    big_read,
    small_read,
    out,
    all_q,
    all_k,
    all_w,
    few_q,
    few_k,
    few_v,
    own_v,
    read_big,
    read_small,
    ready_w,
    small_part,
    latent,
    first_stage,
    stage,
    arrived,
    swap,
    guide,
    near,
    own_sem,
    big_send,
    big_recv,
    value_sem,
    few_send,
    few_recv,
    back_sem,
    swap_sem,
):
    group = lax.axis_index("groups")
    me = lax.axis_index("seq")
    core = lax.axis_index("head")
    host = m - 1
    rungs = n // 2
    rung, side = lax.div(me, 2), lax.rem(me, 2)
    rows = big_q.shape[0]
    tokens = n * rows
    width = all_q.shape[1]
    few_rows = small_q.shape[0]
    few_width = few_q.shape[1]
    heads_here = width // DH
    lat = big_read.shape[0]
    half = rows // 2
    part = half // m

    def window(ref, index, size):
        return ref.at[:, pl.ds(pl.multiple_of(index * size, size), size)]

    def row_block(ref, index, size):
        return ref.at[pl.ds(pl.multiple_of(index * size, size), size), :]

    def toward(distance, act, crossing=None):
        for up in sorted(range(1 - rungs, rungs), key=lambda up: -abs(up)):
            if distance - abs(up) not in (0, 1):
                continue
            there = rung + up
            wanted = (there >= 0) & (there < rungs)
            if crossing is not None:
                other = (rung < rungs // 2) != (there < rungs // 2)
                wanted = wanted & (other if crossing else jnp.logical_not(other))
            peer = there * 2 + lax.rem(side + distance - abs(up), 2)
            pl.when(wanted)(functools.partial(act, peer))

    def chips_at(distance):
        count = 0
        for up in range(1 - rungs, rungs):
            if distance - abs(up) in (0, 1):
                there = rung + up
                count = count + ((there >= 0) & (there < rungs)).astype(jnp.int32)
        return count

    behind = (me != 0).astype(jnp.int32)
    few_pairs = ((small_k, few_k), (small_v, few_v), (small_q, few_q))

    def key_copy(peer):
        return pltpu.make_async_remote_copy(
            src_ref=window(big_k, peer, width),
            dst_ref=row_block(all_k, me, rows),
            send_sem=big_send.at[0],
            recv_sem=big_recv.at[0],
            device_id=(group, peer, core),
            device_id_type=MESH,
        )

    def query_copy(peer):
        return pltpu.make_async_remote_copy(
            src_ref=window(big_q, peer, width),
            dst_ref=row_block(all_q, me, rows),
            send_sem=big_send.at[1],
            recv_sem=big_recv.at[1 + behind],
            device_id=(group, peer, core),
            device_id_type=MESH,
        )

    def value_copy(peer):
        return pltpu.make_async_remote_copy(
            src_ref=ready_w.at[peer],
            dst_ref=row_block(all_w, me, rows),
            send_sem=value_sem.at[0],
            recv_sem=value_sem.at[1],
            device_id=(group, peer, core),
            device_id_type=MESH,
        )

    def few_copy(item, peer):
        source, target = few_pairs[item]
        return pltpu.make_async_remote_copy(
            src_ref=window(source, peer, few_width),
            dst_ref=row_block(target, me * m + core, few_rows),
            send_sem=few_send.at[item],
            recv_sem=few_recv.at[item + behind if item == 2 else item],
            device_id=(group, peer, host),
            device_id_type=MESH,
        )

    def back_copy(peer, which, source):
        return pltpu.make_async_remote_copy(
            src_ref=source,
            dst_ref=arrived.at[me * m + core],
            send_sem=back_sem.at[0],
            recv_sem=back_sem.at[1],
            device_id=(group, peer, which),
            device_id_type=MESH,
        )

    def swap_copy():
        return pltpu.make_async_remote_copy(
            src_ref=swap.at[0],
            dst_ref=swap.at[1],
            send_sem=swap_sem.at[0],
            recv_sem=swap_sem.at[1],
            device_id=(group, me, 1 - core),
            device_id_type=MESH,
        )

    def await_bytes(ref, sem):
        pltpu.make_async_copy(ref, ref, sem).wait()

    barrier = pltpu.get_barrier_semaphore()

    def greet(peer):
        for which in range(m):
            pl.semaphore_signal(
                barrier, inc=1, device_id=(group, peer, which), device_id_type=MESH
            )

    toward(1, greet)
    pl.semaphore_signal(
        barrier, inc=1, device_id=(group, me, 1 - core), device_id_type=MESH
    )

    value_copies = [
        pltpu.make_async_copy(big_v, own_v, own_sem.at[0]),
        pltpu.make_async_copy(big_read, read_big, own_sem.at[1]),
    ]
    for copy in value_copies:
        copy.start()
    late_copies = [
        pltpu.make_async_copy(guidance, guide, own_sem.at[2]),
        pltpu.make_async_copy(window(small_read, me, few_width), read_small, own_sem.at[3]),
    ]
    for copy in late_copies:
        copy.start()
    pltpu.make_async_copy(
        window(big_k, me, width), row_block(all_k, me, rows), big_recv.at[0]
    ).start()

    pltpu.make_async_copy(
        window(big_q, me, width), row_block(all_q, me, rows), big_recv.at[1 + behind]
    ).start()

    @pl.when(core == host)
    def _():
        for item, (source, target) in enumerate(few_pairs):
            pltpu.make_async_copy(
                window(source, me, few_width),
                row_block(target, me * m + host, few_rows),
                few_recv.at[item + behind if item == 2 else item],
            ).start()

    for copy in value_copies:
        copy.wait()
    for seq in range(n):
        terms = []
        for head in range(heads_here):
            columns = slice(seq * width + head * DH, seq * width + (head + 1) * DH)
            terms.append(read_out(own_v[:, columns], read_big[:, columns]))
        ready_w[seq] = jnp.concatenate(terms, axis=1).astype(ready_w.dtype)

    def start_queries(peer):
        few_copy(2, peer).start()
        query_copy(peer).start()

    def start_early(peer):
        for item in (0, 1):
            few_copy(item, peer).start()
        key_copy(peer).start()
        value_copy(peer).start()
        pl.when(me == 0)(functools.partial(start_queries, peer))

    def start_late(peer):
        pl.when(me != 0)(functools.partial(start_queries, peer))

    def pass_on(index):
        def act(peer):
            pl.semaphore_signal(
                near.at[index], inc=1, device_id=(group, peer, core), device_id_type=MESH
            )

        return act

    pl.semaphore_wait(barrier, m * chips_at(1) + m - 1)
    toward(1, pass_on(0))
    toward(1, start_early, True)
    toward(1, start_late, True)
    toward(1, start_early, False)
    known, index = 1, 0
    while known < rungs:
        pl.semaphore_wait(near.at[index], chips_at(known))
        reach = min(2 * known, rungs)
        index += 1
        if reach < rungs:
            toward(reach, pass_on(index))
        for distance in range(known + 1, reach + 1):
            toward(distance, start_early, True)
            toward(distance, start_early, False)
        held, known = known, reach
    for distance in range(held + 1, rungs + 1):
        toward(distance, start_late)
    for distance in range(held, 1, -1):
        toward(distance, start_late)
    toward(1, start_late, False)

    @pl.when(core != host)
    def _():
        for item in range(3):
            few_copy(item, me).start()

    all_w[pl.ds(pl.multiple_of(me * rows, rows), rows), :] = ready_w[me]
    for copy in late_copies:
        copy.wait()
    weight_value = guide[0]

    def attend_rows(first, count, few_waits, head_waits):
        block = pl.ds(first, count)
        lanes = lax.broadcasted_iota(jnp.int32, (count, 2 * lat), 1)

        @pl.when(core == host)
        def _():
            few_waits()
            probs, totals = softmax_parts(few_q[block, :], few_k[...])
            attended = jnp.dot(probs, few_v[...], preferred_element_type=jnp.float32) / totals
            term = read_out(attended.astype(few_v.dtype), read_small[...])
            small_part[block, :] = weight_value * jnp.concatenate(
                [term, jnp.zeros_like(term)], axis=1
            )

        @pl.when(core != host)
        def _():
            small_part[block, :] = jnp.zeros((count, 2 * lat), jnp.float32)

        for head in range(heads_here):
            head_waits(head)
            columns = slice(head * DH, (head + 1) * DH)
            probs, totals = softmax_parts(all_q[block, columns], all_k[:, columns])
            term = jnp.dot(probs, all_w[...], preferred_element_type=jnp.float32) / totals
            term = (1.0 + weight_value) * term
            if head == 0:
                small_part[block, :] = term - small_part[block, :]
        term = jnp.where(lanes < lat, small_part[block, :], term)
        latent[block, :] = term + pltpu.roll(term, lat, 1)
        pair_rows = count // 2
        even = latent[pl.ds(first, pair_rows, stride=2), :]
        odd = latent[pl.ds(first + 1, pair_rows, stride=2), :]
        return jnp.where(lanes[:pair_rows] < lat, even, odd)

    later = tokens - rows

    def first_few_waits():
        await_bytes(few_q.at[pl.ds(0, rows), :], few_recv.at[2])

    def later_few_waits():
        await_bytes(few_q.at[pl.ds(0, later), :], few_recv.at[3])

    def first_head_waits(head):
        if head == 0:
            await_bytes(all_q.at[pl.ds(0, rows), :], big_recv.at[1])

    def later_head_waits(head):
        if head == 0:
            await_bytes(all_q.at[pl.ds(0, later), :], big_recv.at[2])

    def attend_first():
        first_stage[...] = attend_rows(0, rows, first_few_waits, first_head_waits).reshape(
            m, part, 2 * lat
        )

    @pl.when(core == host)
    def _():
        for item in (0, 1):
            await_bytes(few_pairs[item][1], few_recv.at[item])

    await_bytes(all_k, big_recv.at[0])
    await_bytes(all_w.at[pl.ds(0, later), :], value_sem.at[1])

    @pl.when(me != 0)
    def _():
        attend_first()
        for which in range(m):
            back_copy(0, which, first_stage.at[which]).start()

    stage[...] = attend_rows(rows, later, later_few_waits, later_head_waits).reshape(
        (n - 1) * m, part, 2 * lat
    )

    def start_back(peer):
        @pl.when(peer != 0)
        def _():
            for which in range(m):
                back_copy(peer, which, stage.at[(peer - 1) * m + which]).start()

    for distance in range(rungs, 0, -1):
        toward(distance, start_back)

    @pl.when(me != 0)
    def _():
        own = (me - 1) * m
        arrived[me * m + core] = stage[own + core]
        back_copy(me, 1 - core, stage.at[own + 1 - core]).start()

    @pl.when(me == 0)
    def _():
        attend_first()
        arrived[core] = first_stage[core]
        back_copy(0, 1 - core, first_stage.at[1 - core]).start()

    everyone = arrived.at[pl.ds(0, n * m - 1)]
    await_bytes(everyone, back_sem.at[1])
    swap[0] = jnp.sum(arrived[...], axis=0)
    swap_copy().start()
    out[pl.ds(pl.multiple_of(core * part, part), part), :] = swap[0]

    await_bytes(all_k.at[pl.ds(0, later), :], big_send.at[0])
    await_bytes(all_q.at[pl.ds(0, later), :], big_send.at[1])
    await_bytes(all_w.at[pl.ds(0, later), :], value_sem.at[0])
    await_bytes(everyone, back_sem.at[0])

    @pl.when(core == host)
    def _():
        for item in range(3):
            await_bytes(few_pairs[item][1].at[pl.ds(0, (n - 1) * few_rows), :], few_send.at[item])

    @pl.when(core != host)
    def _():
        for item in range(3):
            await_bytes(few_pairs[item][1].at[pl.ds(0, n * few_rows), :], few_send.at[item])

    swap_copy().wait()
    out[pl.ds(pl.multiple_of((1 - core) * part, part), part), :] = swap[1]


def fused(
    n,
    m,
    big_queries,
    big_keys,
    big_values,
    small_queries,
    small_keys,
    small_values,
    big_readout,
    small_readout,
    guidance,
):
    rows, columns = big_queries.shape
    few_rows, few_columns = small_queries.shape
    width, few_width = columns // n, few_columns // n
    tokens = rows * n
    lat = big_readout.shape[1]
    half = rows // 2
    part = half // m
    kind = jnp.bfloat16
    dma = pltpu.SemaphoreType.DMA
    return pl.pallas_call(
        functools.partial(window_kernel, n, m),
        out_shape=pltpu.VMEM((half, 2 * lat), jnp.float32),
        in_specs=[pl.BlockSpec(memory_space=pl.ANY)] * 9,
        out_specs=pl.BlockSpec(memory_space=pltpu.VMEM),
        scratch_shapes=[
            pltpu.VMEM((tokens, width), kind),
            pltpu.VMEM((tokens, width), kind),
            pltpu.VMEM((tokens, 2 * lat), kind),
            pltpu.VMEM((tokens, few_width), kind),
            pltpu.VMEM((tokens, few_width), kind),
            pltpu.VMEM((tokens, few_width), kind),
            pltpu.VMEM((rows, columns), kind),
            pltpu.VMEM((lat, columns), kind),
            pltpu.VMEM((lat, few_width), kind),
            pltpu.VMEM((n, rows, 2 * lat), kind),
            pltpu.VMEM((tokens, 2 * lat), jnp.float32),
            pltpu.VMEM((tokens, 2 * lat), jnp.float32),
            pltpu.VMEM((m, part, 2 * lat), jnp.float32),
            pltpu.VMEM(((n - 1) * m, part, 2 * lat), jnp.float32),
            pltpu.VMEM((n * m, part, 2 * lat), jnp.float32),
            pltpu.VMEM((2, part, 2 * lat), jnp.float32),
            pltpu.SMEM((1,), jnp.float32),
            pltpu.SemaphoreType.REGULAR(((n // 2 - 1).bit_length(),)),
            dma((4,)),
            dma((2,)),
            dma((3,)),
            dma((2,)),
            dma((3,)),
            dma((4,)),
            dma((2,)),
            dma((2,)),
        ],
        compiler_params=pltpu.CompilerParams(collective_id=0, has_side_effects=True),
        name="fused_window",
    )(
        guidance,
        big_queries,
        big_keys,
        big_values,
        small_queries,
        small_keys,
        small_values,
        big_readout.T,
        small_readout.T,
    )


def fits(n, m, big_queries, small_queries, lat):
    rows, columns = big_queries.shape
    few_rows, few_columns = small_queries.shape
    return (
        n > 2
        and n % 2 == 0
        and m == 2
        and n * rows <= 512
        and columns == 2 * n * DH
        and few_columns == n * DH
        and rows == m * few_rows
        and few_rows % 16 == 0
        and 2 * lat == 128
    )


def shards(*arguments):
    n, m = lax.axis_size("seq"), lax.axis_size("head")
    if fits(n, m, arguments[0], arguments[3], arguments[6].shape[1]):
        return fused(n, m, *arguments)
    return exchanged(*arguments)


def solution(mesh):
    placed = (
        P(("groups", "seq"), "head"),
        P(("groups", "seq"), "head"),
        P(("groups", "seq"), "head"),
        P(("groups", "seq", "head"), None),
        P(("groups", "seq", "head"), None),
        P(("groups", "seq", "head"), None),
        P("head", None),
        P(),
        P("groups"),
    )
    return jax.shard_map(
        shards, mesh=mesh, in_specs=placed, out_specs=P(("groups", "seq"), None), check_vma=False
    )
```

```python
import functools
import math

import jax
import jax.numpy as jnp
from jax import lax
from jax.experimental import pallas as pl
from jax.experimental.pallas import tpu as pltpu
from jax.sharding import PartitionSpec as P

DH = 128


def split_heads(matrix, blocks, parts):
    rows_here, columns = matrix.shape
    shaped = matrix.reshape(blocks, rows_here // blocks, parts, columns // parts)
    shaped = jnp.transpose(shaped, (0, 2, 1, 3))
    return shaped.reshape(blocks * parts, rows_here // blocks, columns // parts)


def copy_heads(matrix, blocks, parts):
    rows_here, columns = matrix.shape
    shaped = jnp.transpose(matrix.reshape(rows_here, parts, columns // parts), (1, 0, 2))
    shaped = jnp.broadcast_to(shaped[None], (blocks, parts, rows_here, columns // parts))
    return shaped.reshape(blocks * parts, rows_here, columns // parts)


def join_heads(stacked, blocks, parts):
    pieces, rows_here, columns = stacked.shape
    shaped = stacked.reshape(blocks, parts, rows_here, columns)
    shaped = jnp.transpose(shaped, (0, 2, 1, 3))
    return shaped.reshape(blocks * rows_here, parts * columns)


def attend(query_rows, key_rows, value_rows):
    query_count = query_rows.shape[0]
    heads_here = query_rows.shape[1] // DH
    key_count = key_rows.shape[0]
    block_height = math.gcd(query_count, 256)
    block_count = query_count // block_height
    query_blocks = query_rows.reshape(block_count, block_height, heads_here, DH)
    key_split = key_rows.reshape(key_count, heads_here, DH)
    value_split = value_rows.reshape(key_count, heads_here, DH)
    score_scale = 1.0 / math.sqrt(DH)

    def one_block(query_block):
        scores = (
            jnp.einsum("qgd,kgd->gqk", query_block, key_split, preferred_element_type=jnp.float32)
            * score_scale
        )
        row_max = jnp.max(scores, axis=2, keepdims=True)
        probs = jnp.exp(scores - row_max)
        totals = jnp.sum(probs, axis=2, keepdims=True)
        weights = probs.astype(jnp.bfloat16)
        accumulated = jnp.einsum(
            "gqk,kgd->gqd", weights, value_split, preferred_element_type=jnp.float32
        )
        attended = accumulated / totals
        attended = jnp.transpose(attended, (1, 0, 2)).reshape(block_height, heads_here * DH)
        return attended.astype(jnp.bfloat16)

    outputs = lax.map(one_block, query_blocks)
    return outputs.reshape(query_count, heads_here * DH)


def exchanged(
    big_queries,
    big_keys,
    big_values,
    small_queries,
    small_keys,
    small_values,
    big_readout,
    small_readout,
    guidance,
):
    seq_count = lax.axis_size("seq")
    big_heads = big_queries.shape[1] // DH
    big_group = max(big_heads // seq_count, 1)
    big_blocks = max(seq_count // big_heads, 1)
    big_parts = big_heads // big_group
    query_rows = lax.all_to_all(
        split_heads(big_queries, big_blocks, big_parts),
        "seq",
        split_axis=0,
        concat_axis=1,
        tiled=True,
    )[0]
    key_copies, value_copies = (
        lax.all_to_all(
            copy_heads(big_keys, big_blocks, big_parts),
            "seq",
            split_axis=0,
            concat_axis=1,
            tiled=True,
        ),
        lax.all_to_all(
            copy_heads(big_values, big_blocks, big_parts),
            "seq",
            split_axis=0,
            concat_axis=1,
            tiled=True,
        ),
    )
    key_rows = key_copies[0]
    value_rows = value_copies[0]
    big_out = attend(query_rows, key_rows, value_rows)
    big_back = lax.all_to_all(big_out[None], "seq", split_axis=1, concat_axis=0, tiled=True)
    big_attention = join_heads(big_back, big_blocks, big_parts)
    big_partial = jnp.dot(big_attention, big_readout, preferred_element_type=jnp.float32)
    small_heads = small_queries.shape[1] // DH
    small_group = max(small_heads // seq_count, 1)
    small_blocks = max(seq_count // small_heads, 1)
    small_parts = small_heads // small_group
    small_query_rows = lax.all_to_all(
        split_heads(small_queries, small_blocks, small_parts),
        "seq",
        split_axis=0,
        concat_axis=1,
        tiled=True,
    )[0]
    key_copies, value_copies = (
        lax.all_to_all(
            copy_heads(small_keys, small_blocks, small_parts),
            "seq",
            split_axis=0,
            concat_axis=1,
            tiled=True,
        ),
        lax.all_to_all(
            copy_heads(small_values, small_blocks, small_parts),
            "seq",
            split_axis=0,
            concat_axis=1,
            tiled=True,
        ),
    )
    small_key_rows, small_value_rows = (
        lax.all_gather(key_copies[0], "head", axis=0, tiled=True),
        lax.all_gather(value_copies[0], "head", axis=0, tiled=True),
    )
    small_out = attend(small_query_rows, small_key_rows, small_value_rows)
    small_back = lax.all_to_all(small_out[None], "seq", split_axis=1, concat_axis=0, tiled=True)
    small_attention = join_heads(small_back, small_blocks, small_parts)
    small_latent = jnp.dot(small_attention, small_readout, preferred_element_type=jnp.float32)
    weight_value = guidance[0]
    core_index = lax.axis_index("head")
    placed = lax.dynamic_update_slice(
        jnp.zeros_like(big_partial),
        small_latent,
        (core_index * small_latent.shape[0], jnp.zeros((), jnp.int32)),
    )
    blended = lax.psum((1.0 + weight_value) * big_partial - weight_value * placed, "head")
    return blended.reshape(blended.shape[0] // 2, 2 * blended.shape[1])


MESH = pl.DeviceIdType.MESH


def softmax_parts(query_head, key_head):
    scores = lax.dot_general(
        query_head, key_head, (((1,), (1,)), ((), ())), preferred_element_type=jnp.float32
    ) * (1.0 / math.sqrt(DH))
    row_max = jnp.max(scores, axis=1, keepdims=True)
    probs = jnp.exp(scores - row_max)
    totals = jnp.sum(probs, axis=1, keepdims=True)
    return probs.astype(jnp.bfloat16), totals


def read_out(values, readout):
    return lax.dot_general(
        values, readout, (((1,), (1,)), ((), ())), preferred_element_type=jnp.float32
    )


def window_kernel(
    n,
    m,
    guidance,
    big_q,
    big_k,
    big_v,
    small_q,
    small_k,
    small_v,
    big_read,
    small_read,
    out,
    all_q,
    all_k,
    all_w,
    few_q,
    few_k,
    few_w,
    own_v,
    own_few_v,
    read_big,
    read_small,
    ready_w,
    ready_few,
    small_part,
    latent,
    first_stage,
    stage,
    arrived,
    swap,
    guide,
    near,
    own_sem,
    big_send,
    big_recv,
    value_sem,
    few_send,
    few_recv,
    back_sem,
    swap_sem,
):
    group = lax.axis_index("groups")
    me = lax.axis_index("seq")
    core = lax.axis_index("head")
    host = m - 1
    rungs = n // 2
    rung, side = lax.div(me, 2), lax.rem(me, 2)
    rows = big_q.shape[0]
    tokens = n * rows
    width = all_q.shape[1]
    few_rows = small_q.shape[0]
    few_width = few_q.shape[1]
    heads_here = width // DH
    lat = big_read.shape[0]
    half = rows // 2
    part = half // m

    def window(ref, index, size):
        return ref.at[:, pl.ds(pl.multiple_of(index * size, size), size)]

    def row_block(ref, index, size):
        return ref.at[pl.ds(pl.multiple_of(index * size, size), size), :]

    def toward(distance, act, crossing=None):
        for up in sorted(range(1 - rungs, rungs), key=lambda up: -abs(up)):
            if distance - abs(up) not in (0, 1):
                continue
            there = rung + up
            wanted = (there >= 0) & (there < rungs)
            if crossing is not None:
                other = (rung < rungs // 2) != (there < rungs // 2)
                wanted = wanted & (other if crossing else jnp.logical_not(other))
            peer = there * 2 + lax.rem(side + distance - abs(up), 2)
            pl.when(wanted)(functools.partial(act, peer))

    def chips_at(distance):
        count = 0
        for up in range(1 - rungs, rungs):
            if distance - abs(up) in (0, 1):
                there = rung + up
                count = count + ((there >= 0) & (there < rungs)).astype(jnp.int32)
        return count

    behind = (me != 0).astype(jnp.int32)
    few_pairs = ((small_k, few_k), (ready_few, few_w), (small_q, few_q))

    def key_copy(peer):
        return pltpu.make_async_remote_copy(
            src_ref=window(big_k, peer, width),
            dst_ref=row_block(all_k, me, rows),
            send_sem=big_send.at[0],
            recv_sem=big_recv.at[0],
            device_id=(group, peer, core),
            device_id_type=MESH,
        )

    def query_copy(peer):
        return pltpu.make_async_remote_copy(
            src_ref=window(big_q, peer, width),
            dst_ref=row_block(all_q, me, rows),
            send_sem=big_send.at[1],
            recv_sem=big_recv.at[1 + behind],
            device_id=(group, peer, core),
            device_id_type=MESH,
        )

    def value_copy(peer):
        return pltpu.make_async_remote_copy(
            src_ref=ready_w.at[peer],
            dst_ref=row_block(all_w, me, rows),
            send_sem=value_sem.at[0],
            recv_sem=value_sem.at[1],
            device_id=(group, peer, core),
            device_id_type=MESH,
        )

    def few_copy(item, peer):
        source, target = few_pairs[item]
        return pltpu.make_async_remote_copy(
            src_ref=source.at[peer] if item == 1 else window(source, peer, few_width),
            dst_ref=(
                target.at[me * m + core]
                if item == 1
                else row_block(target, me * m + core, few_rows)
            ),
            send_sem=few_send.at[item],
            recv_sem=few_recv.at[item + behind if item == 2 else item],
            device_id=(group, peer, host),
            device_id_type=MESH,
        )

    def back_copy(peer, which, source):
        return pltpu.make_async_remote_copy(
            src_ref=source,
            dst_ref=arrived.at[me * m + core],
            send_sem=back_sem.at[0],
            recv_sem=back_sem.at[1],
            device_id=(group, peer, which),
            device_id_type=MESH,
        )

    def swap_copy():
        return pltpu.make_async_remote_copy(
            src_ref=swap.at[0],
            dst_ref=swap.at[1],
            send_sem=swap_sem.at[0],
            recv_sem=swap_sem.at[1],
            device_id=(group, me, 1 - core),
            device_id_type=MESH,
        )

    def await_bytes(ref, sem):
        pltpu.make_async_copy(ref, ref, sem).wait()

    barrier = pltpu.get_barrier_semaphore()

    def greet(peer):
        for which in range(m):
            pl.semaphore_signal(
                barrier, inc=1, device_id=(group, peer, which), device_id_type=MESH
            )

    toward(1, greet)
    pl.semaphore_signal(
        barrier, inc=1, device_id=(group, me, 1 - core), device_id_type=MESH
    )

    value_copies = [
        pltpu.make_async_copy(big_v, own_v, own_sem.at[0]),
        pltpu.make_async_copy(big_read, read_big, own_sem.at[1]),
        pltpu.make_async_copy(small_v, own_few_v, own_sem.at[2]),
        pltpu.make_async_copy(small_read, read_small, own_sem.at[3]),
    ]
    for copy in value_copies:
        copy.start()
    guide_copy = pltpu.make_async_copy(guidance, guide, own_sem.at[4])
    guide_copy.start()
    pltpu.make_async_copy(
        window(big_k, me, width), row_block(all_k, me, rows), big_recv.at[0]
    ).start()

    pltpu.make_async_copy(
        window(big_q, me, width), row_block(all_q, me, rows), big_recv.at[1 + behind]
    ).start()

    @pl.when(core == host)
    def _():
        for item in (0, 2):
            source, target = few_pairs[item]
            pltpu.make_async_copy(
                window(source, me, few_width),
                row_block(target, me * m + host, few_rows),
                few_recv.at[item + behind if item == 2 else item],
            ).start()

    for copy in value_copies:
        copy.wait()
    for seq in range(n):
        terms = []
        for head in range(heads_here):
            columns = slice(seq * width + head * DH, seq * width + (head + 1) * DH)
            terms.append(read_out(own_v[:, columns], read_big[:, columns]))
        ready_w[seq] = jnp.concatenate(terms, axis=1).astype(ready_w.dtype)
        columns = slice(seq * few_width, (seq + 1) * few_width)
        term = read_out(own_few_v[:, columns], read_small[:, columns])
        term = jnp.concatenate([term[: few_rows // 2], term[few_rows // 2 :]], axis=1)
        ready_few[seq] = term.astype(ready_few.dtype)

    def start_queries(peer):
        few_copy(2, peer).start()
        query_copy(peer).start()

    def start_early(peer):
        for item in (0, 1):
            few_copy(item, peer).start()
        key_copy(peer).start()
        value_copy(peer).start()
        pl.when(me == 0)(functools.partial(start_queries, peer))

    def start_late(peer):
        pl.when(me != 0)(functools.partial(start_queries, peer))

    def pass_on(index):
        def act(peer):
            pl.semaphore_signal(
                near.at[index], inc=1, device_id=(group, peer, core), device_id_type=MESH
            )

        return act

    pl.semaphore_wait(barrier, m * chips_at(1) + m - 1)
    toward(1, pass_on(0))
    toward(1, start_early, True)
    toward(1, start_early, False)
    known, index = 1, 0
    while known < rungs:
        pl.semaphore_wait(near.at[index], chips_at(known))
        reach = min(2 * known, rungs)
        index += 1
        if reach < rungs:
            toward(reach, pass_on(index))
        for distance in range(known + 1, reach + 1):
            toward(distance, start_early, True)
            toward(distance, start_early, False)
        held, known = known, reach
    for distance in range(held + 1, rungs + 1):
        toward(distance, start_late)
    for distance in range(held, 0, -1):
        toward(distance, start_late)

    @pl.when(core != host)
    def _():
        for item in range(3):
            few_copy(item, me).start()

    all_w[pl.ds(pl.multiple_of(me * rows, rows), rows), :] = ready_w[me]
    guide_copy.wait()
    weight_value = guide[0]

    def attend_rows(first, count, few_waits, head_waits):
        block = pl.ds(first, count)
        lanes = lax.broadcasted_iota(jnp.int32, (count, 2 * lat), 1)

        @pl.when(core == host)
        def _():
            few_waits()
            probs, totals = softmax_parts(few_q[block, :], few_k[...])
            pairs = few_w[...].astype(jnp.float32).reshape(n * m * few_rows // 2, 2 * lat)
            sides = [
                side.reshape(n * m, few_rows // 2, 2 * lat)
                for side in (pairs, pltpu.roll(pairs, lat, 1))
            ]
            held = jnp.concatenate(sides, axis=1).reshape(tokens, 2 * lat)
            term = jnp.dot(probs, held.astype(few_w.dtype), preferred_element_type=jnp.float32)
            small_part[block, :] = weight_value * term / totals

        @pl.when(core != host)
        def _():
            small_part[block, :] = jnp.zeros((count, 2 * lat), jnp.float32)

        for head in range(heads_here):
            head_waits(head)
            columns = slice(head * DH, (head + 1) * DH)
            probs, totals = softmax_parts(all_q[block, columns], all_k[:, columns])
            term = jnp.dot(probs, all_w[...], preferred_element_type=jnp.float32) / totals
            term = (1.0 + weight_value) * term
            if head == 0:
                small_part[block, :] = term - small_part[block, :]
        term = jnp.where(lanes < lat, small_part[block, :], term)
        latent[block, :] = term + pltpu.roll(term, lat, 1)
        pair_rows = count // 2
        even = latent[pl.ds(first, pair_rows, stride=2), :]
        odd = latent[pl.ds(first + 1, pair_rows, stride=2), :]
        return jnp.where(lanes[:pair_rows] < lat, even, odd)

    later = tokens - rows

    def first_few_waits():
        await_bytes(few_q.at[pl.ds(0, rows), :], few_recv.at[2])

    def later_few_waits():
        await_bytes(few_q.at[pl.ds(0, later), :], few_recv.at[3])

    def first_head_waits(head):
        if head == 0:
            await_bytes(all_q.at[pl.ds(0, rows), :], big_recv.at[1])

    def later_head_waits(head):
        if head == 0:
            await_bytes(all_q.at[pl.ds(0, later), :], big_recv.at[2])

    def attend_first():
        first_stage[...] = attend_rows(0, rows, first_few_waits, first_head_waits).reshape(
            m, part, 2 * lat
        )

    @pl.when(core == host)
    def _():
        few_w[me * m + host] = ready_few[me]
        await_bytes(few_k, few_recv.at[0])
        await_bytes(few_w.at[pl.ds(0, n * m - 1)], few_recv.at[1])

    await_bytes(all_k, big_recv.at[0])
    await_bytes(all_w.at[pl.ds(0, later), :], value_sem.at[1])

    @pl.when(me != 0)
    def _():
        attend_first()
        for which in range(m):
            back_copy(0, which, first_stage.at[which]).start()

    stage[...] = attend_rows(rows, later, later_few_waits, later_head_waits).reshape(
        (n - 1) * m, part, 2 * lat
    )

    def start_back(peer):
        @pl.when(peer != 0)
        def _():
            for which in range(m):
                back_copy(peer, which, stage.at[(peer - 1) * m + which]).start()

    for distance in range(rungs, 0, -1):
        toward(distance, start_back)

    @pl.when(me != 0)
    def _():
        own = (me - 1) * m
        arrived[me * m + core] = stage[own + core]
        back_copy(me, 1 - core, stage.at[own + 1 - core]).start()

    @pl.when(me == 0)
    def _():
        attend_first()
        arrived[core] = first_stage[core]
        back_copy(0, 1 - core, first_stage.at[1 - core]).start()

    everyone = arrived.at[pl.ds(0, n * m - 1)]
    await_bytes(everyone, back_sem.at[1])
    swap[0] = jnp.sum(arrived[...], axis=0)
    swap_copy().start()
    out[pl.ds(pl.multiple_of(core * part, part), part), :] = swap[0]

    await_bytes(all_k.at[pl.ds(0, later), :], big_send.at[0])
    await_bytes(all_q.at[pl.ds(0, later), :], big_send.at[1])
    await_bytes(all_w.at[pl.ds(0, later), :], value_sem.at[0])
    await_bytes(everyone, back_sem.at[0])

    def await_few(chips):
        for item in (0, 2):
            await_bytes(few_pairs[item][1].at[pl.ds(0, chips * few_rows), :], few_send.at[item])
        await_bytes(few_w.at[pl.ds(0, chips)], few_send.at[1])

    pl.when(core == host)(functools.partial(await_few, n - 1))
    pl.when(core != host)(functools.partial(await_few, n))

    swap_copy().wait()
    out[pl.ds(pl.multiple_of((1 - core) * part, part), part), :] = swap[1]


def fused(
    n,
    m,
    big_queries,
    big_keys,
    big_values,
    small_queries,
    small_keys,
    small_values,
    big_readout,
    small_readout,
    guidance,
):
    rows, columns = big_queries.shape
    few_rows, few_columns = small_queries.shape
    width, few_width = columns // n, few_columns // n
    tokens = rows * n
    lat = big_readout.shape[1]
    half = rows // 2
    part = half // m
    kind = jnp.bfloat16
    dma = pltpu.SemaphoreType.DMA
    return pl.pallas_call(
        functools.partial(window_kernel, n, m),
        out_shape=pltpu.VMEM((half, 2 * lat), jnp.float32),
        in_specs=[pl.BlockSpec(memory_space=pl.ANY)] * 9,
        out_specs=pl.BlockSpec(memory_space=pltpu.VMEM),
        scratch_shapes=[
            pltpu.VMEM((tokens, width), kind),
            pltpu.VMEM((tokens, width), kind),
            pltpu.VMEM((tokens, 2 * lat), kind),
            pltpu.VMEM((tokens, few_width), kind),
            pltpu.VMEM((tokens, few_width), kind),
            pltpu.VMEM((n * m, few_rows // 2, 2 * lat), kind),
            pltpu.VMEM((rows, columns), kind),
            pltpu.VMEM((few_rows, few_columns), kind),
            pltpu.VMEM((lat, columns), kind),
            pltpu.VMEM((lat, few_columns), kind),
            pltpu.VMEM((n, rows, 2 * lat), kind),
            pltpu.VMEM((n, few_rows // 2, 2 * lat), kind),
            pltpu.VMEM((tokens, 2 * lat), jnp.float32),
            pltpu.VMEM((tokens, 2 * lat), jnp.float32),
            pltpu.VMEM((m, part, 2 * lat), jnp.float32),
            pltpu.VMEM(((n - 1) * m, part, 2 * lat), jnp.float32),
            pltpu.VMEM((n * m, part, 2 * lat), jnp.float32),
            pltpu.VMEM((2, part, 2 * lat), jnp.float32),
            pltpu.SMEM((1,), jnp.float32),
            pltpu.SemaphoreType.REGULAR(((n // 2 - 1).bit_length(),)),
            dma((5,)),
            dma((2,)),
            dma((3,)),
            dma((2,)),
            dma((3,)),
            dma((4,)),
            dma((2,)),
            dma((2,)),
        ],
        compiler_params=pltpu.CompilerParams(collective_id=0, has_side_effects=True),
        name="fused_window",
    )(
        guidance,
        big_queries,
        big_keys,
        big_values,
        small_queries,
        small_keys,
        small_values,
        big_readout.T,
        small_readout.T,
    )


def fits(n, m, big_queries, small_queries, lat):
    rows, columns = big_queries.shape
    few_rows, few_columns = small_queries.shape
    return (
        n > 2
        and n % 2 == 0
        and m == 2
        and n * rows <= 512
        and columns == 2 * n * DH
        and few_columns == n * DH
        and rows == m * few_rows
        and few_rows % 16 == 0
        and 2 * lat == 128
    )


def shards(*arguments):
    n, m = lax.axis_size("seq"), lax.axis_size("head")
    if fits(n, m, arguments[0], arguments[3], arguments[6].shape[1]):
        return fused(n, m, *arguments)
    return exchanged(*arguments)


def solution(mesh):
    placed = (
        P(("groups", "seq"), "head"),
        P(("groups", "seq"), "head"),
        P(("groups", "seq"), "head"),
        P(("groups", "seq", "head"), None),
        P(("groups", "seq", "head"), None),
        P(("groups", "seq", "head"), None),
        P("head", None),
        P(),
        P("groups"),
    )
    return jax.shard_map(
        shards, mesh=mesh, in_specs=placed, out_specs=P(("groups", "seq"), None), check_vma=False
    )
```

```python
import functools
import math

import jax
import jax.numpy as jnp
from jax import lax
from jax.experimental import pallas as pl
from jax.experimental.pallas import tpu as pltpu
from jax.sharding import PartitionSpec as P

DH = 128


def split_heads(matrix, blocks, parts):
    rows_here, columns = matrix.shape
    shaped = matrix.reshape(blocks, rows_here // blocks, parts, columns // parts)
    shaped = jnp.transpose(shaped, (0, 2, 1, 3))
    return shaped.reshape(blocks * parts, rows_here // blocks, columns // parts)


def copy_heads(matrix, blocks, parts):
    rows_here, columns = matrix.shape
    shaped = jnp.transpose(matrix.reshape(rows_here, parts, columns // parts), (1, 0, 2))
    shaped = jnp.broadcast_to(shaped[None], (blocks, parts, rows_here, columns // parts))
    return shaped.reshape(blocks * parts, rows_here, columns // parts)


def join_heads(stacked, blocks, parts):
    pieces, rows_here, columns = stacked.shape
    shaped = stacked.reshape(blocks, parts, rows_here, columns)
    shaped = jnp.transpose(shaped, (0, 2, 1, 3))
    return shaped.reshape(blocks * rows_here, parts * columns)


def attend(query_rows, key_rows, value_rows):
    query_count = query_rows.shape[0]
    heads_here = query_rows.shape[1] // DH
    key_count = key_rows.shape[0]
    block_height = math.gcd(query_count, 256)
    block_count = query_count // block_height
    query_blocks = query_rows.reshape(block_count, block_height, heads_here, DH)
    key_split = key_rows.reshape(key_count, heads_here, DH)
    value_split = value_rows.reshape(key_count, heads_here, DH)
    score_scale = 1.0 / math.sqrt(DH)

    def one_block(query_block):
        scores = (
            jnp.einsum("qgd,kgd->gqk", query_block, key_split, preferred_element_type=jnp.float32)
            * score_scale
        )
        row_max = jnp.max(scores, axis=2, keepdims=True)
        probs = jnp.exp(scores - row_max)
        totals = jnp.sum(probs, axis=2, keepdims=True)
        weights = probs.astype(jnp.bfloat16)
        accumulated = jnp.einsum(
            "gqk,kgd->gqd", weights, value_split, preferred_element_type=jnp.float32
        )
        attended = accumulated / totals
        attended = jnp.transpose(attended, (1, 0, 2)).reshape(block_height, heads_here * DH)
        return attended.astype(jnp.bfloat16)

    outputs = lax.map(one_block, query_blocks)
    return outputs.reshape(query_count, heads_here * DH)


def exchanged(
    big_queries,
    big_keys,
    big_values,
    small_queries,
    small_keys,
    small_values,
    big_readout,
    small_readout,
    guidance,
):
    seq_count = lax.axis_size("seq")
    big_heads = big_queries.shape[1] // DH
    big_group = max(big_heads // seq_count, 1)
    big_blocks = max(seq_count // big_heads, 1)
    big_parts = big_heads // big_group
    query_rows = lax.all_to_all(
        split_heads(big_queries, big_blocks, big_parts),
        "seq",
        split_axis=0,
        concat_axis=1,
        tiled=True,
    )[0]
    key_copies, value_copies = (
        lax.all_to_all(
            copy_heads(big_keys, big_blocks, big_parts),
            "seq",
            split_axis=0,
            concat_axis=1,
            tiled=True,
        ),
        lax.all_to_all(
            copy_heads(big_values, big_blocks, big_parts),
            "seq",
            split_axis=0,
            concat_axis=1,
            tiled=True,
        ),
    )
    key_rows = key_copies[0]
    value_rows = value_copies[0]
    big_out = attend(query_rows, key_rows, value_rows)
    big_back = lax.all_to_all(big_out[None], "seq", split_axis=1, concat_axis=0, tiled=True)
    big_attention = join_heads(big_back, big_blocks, big_parts)
    big_partial = jnp.dot(big_attention, big_readout, preferred_element_type=jnp.float32)
    small_heads = small_queries.shape[1] // DH
    small_group = max(small_heads // seq_count, 1)
    small_blocks = max(seq_count // small_heads, 1)
    small_parts = small_heads // small_group
    small_query_rows = lax.all_to_all(
        split_heads(small_queries, small_blocks, small_parts),
        "seq",
        split_axis=0,
        concat_axis=1,
        tiled=True,
    )[0]
    key_copies, value_copies = (
        lax.all_to_all(
            copy_heads(small_keys, small_blocks, small_parts),
            "seq",
            split_axis=0,
            concat_axis=1,
            tiled=True,
        ),
        lax.all_to_all(
            copy_heads(small_values, small_blocks, small_parts),
            "seq",
            split_axis=0,
            concat_axis=1,
            tiled=True,
        ),
    )
    small_key_rows, small_value_rows = (
        lax.all_gather(key_copies[0], "head", axis=0, tiled=True),
        lax.all_gather(value_copies[0], "head", axis=0, tiled=True),
    )
    small_out = attend(small_query_rows, small_key_rows, small_value_rows)
    small_back = lax.all_to_all(small_out[None], "seq", split_axis=1, concat_axis=0, tiled=True)
    small_attention = join_heads(small_back, small_blocks, small_parts)
    small_latent = jnp.dot(small_attention, small_readout, preferred_element_type=jnp.float32)
    weight_value = guidance[0]
    core_index = lax.axis_index("head")
    placed = lax.dynamic_update_slice(
        jnp.zeros_like(big_partial),
        small_latent,
        (core_index * small_latent.shape[0], jnp.zeros((), jnp.int32)),
    )
    blended = lax.psum((1.0 + weight_value) * big_partial - weight_value * placed, "head")
    return blended.reshape(blended.shape[0] // 2, 2 * blended.shape[1])


MESH = pl.DeviceIdType.MESH


def softmax_parts(query_head, key_head):
    scores = lax.dot_general(
        query_head, key_head, (((1,), (1,)), ((), ())), preferred_element_type=jnp.float32
    ) * (1.0 / math.sqrt(DH))
    row_max = jnp.max(scores, axis=1, keepdims=True)
    probs = jnp.exp(scores - row_max)
    totals = jnp.sum(probs, axis=1, keepdims=True)
    return probs.astype(jnp.bfloat16), totals


def read_out(values, readout):
    return lax.dot_general(
        values, readout, (((1,), (1,)), ((), ())), preferred_element_type=jnp.float32
    )


def window_kernel(
    n,
    m,
    guidance,
    big_q,
    big_k,
    big_v,
    small_q,
    small_k,
    small_v,
    big_read,
    small_read,
    out,
    all_q,
    all_k,
    all_w,
    few_q,
    few_k,
    few_w,
    own_v,
    own_few_v,
    read_big,
    read_small,
    ready_w,
    ready_few,
    small_part,
    latent,
    first_stage,
    stage,
    first_arrived,
    arrived,
    swap,
    guide,
    near,
    own_sem,
    big_send,
    big_recv,
    value_sem,
    few_send,
    few_recv,
    first_sem,
    back_sem,
    swap_sem,
):
    group = lax.axis_index("groups")
    me = lax.axis_index("seq")
    core = lax.axis_index("head")
    host = m - 1
    rungs = n // 2
    rung, side = lax.div(me, 2), lax.rem(me, 2)
    rows = big_q.shape[0]
    tokens = n * rows
    width = all_q.shape[1]
    few_rows = small_q.shape[0]
    few_width = few_q.shape[1]
    heads_here = width // DH
    lat = big_read.shape[0]
    half = rows // 2
    part = half // m

    def window(ref, index, size):
        return ref.at[:, pl.ds(pl.multiple_of(index * size, size), size)]

    def row_block(ref, index, size):
        return ref.at[pl.ds(pl.multiple_of(index * size, size), size), :]

    def toward(distance, act, crossing=None):
        for up in sorted(range(1 - rungs, rungs), key=lambda up: -abs(up)):
            if distance - abs(up) not in (0, 1):
                continue
            there = rung + up
            wanted = (there >= 0) & (there < rungs)
            if crossing is not None:
                other = (rung < rungs // 2) != (there < rungs // 2)
                wanted = wanted & (other if crossing else jnp.logical_not(other))
            peer = there * 2 + lax.rem(side + distance - abs(up), 2)
            pl.when(wanted)(functools.partial(act, peer))

    def chips_at(distance):
        count = 0
        for up in range(1 - rungs, rungs):
            if distance - abs(up) in (0, 1):
                there = rung + up
                count = count + ((there >= 0) & (there < rungs)).astype(jnp.int32)
        return count

    behind = (me != 0).astype(jnp.int32)
    few_pairs = ((small_k, few_k), (ready_few, few_w), (small_q, few_q))

    def key_copy(peer):
        return pltpu.make_async_remote_copy(
            src_ref=window(big_k, peer, width),
            dst_ref=row_block(all_k, me, rows),
            send_sem=big_send.at[0],
            recv_sem=big_recv.at[0],
            device_id=(group, peer, core),
            device_id_type=MESH,
        )

    def query_copy(peer):
        return pltpu.make_async_remote_copy(
            src_ref=window(big_q, peer, width),
            dst_ref=row_block(all_q, me, rows),
            send_sem=big_send.at[1],
            recv_sem=big_recv.at[1 + behind],
            device_id=(group, peer, core),
            device_id_type=MESH,
        )

    def value_copy(peer):
        return pltpu.make_async_remote_copy(
            src_ref=ready_w.at[peer],
            dst_ref=row_block(all_w, me, rows),
            send_sem=value_sem.at[0],
            recv_sem=value_sem.at[1],
            device_id=(group, peer, core),
            device_id_type=MESH,
        )

    def few_copy(item, peer):
        source, target = few_pairs[item]
        return pltpu.make_async_remote_copy(
            src_ref=source.at[peer] if item == 1 else window(source, peer, few_width),
            dst_ref=(
                target.at[me * m + core]
                if item == 1
                else row_block(target, me * m + core, few_rows)
            ),
            send_sem=few_send.at[item],
            recv_sem=few_recv.at[item + behind if item == 2 else item],
            device_id=(group, peer, host),
            device_id_type=MESH,
        )

    def back_copy(peer, which, source):
        return pltpu.make_async_remote_copy(
            src_ref=source,
            dst_ref=arrived.at[me * m + core],
            send_sem=back_sem.at[0],
            recv_sem=back_sem.at[1],
            device_id=(group, peer, which),
            device_id_type=MESH,
        )

    def first_copy(which):
        return pltpu.make_async_remote_copy(
            src_ref=first_stage,
            dst_ref=first_arrived.at[me * m + core],
            send_sem=first_sem.at[0],
            recv_sem=first_sem.at[1],
            device_id=(group, 0, which),
            device_id_type=MESH,
        )

    def swap_copy():
        return pltpu.make_async_remote_copy(
            src_ref=swap.at[0],
            dst_ref=swap.at[1],
            send_sem=swap_sem.at[0],
            recv_sem=swap_sem.at[1],
            device_id=(group, me, 1 - core),
            device_id_type=MESH,
        )

    def await_bytes(ref, sem):
        pltpu.make_async_copy(ref, ref, sem).wait()

    barrier = pltpu.get_barrier_semaphore()

    def greet(peer):
        for which in range(m):
            pl.semaphore_signal(
                barrier, inc=1, device_id=(group, peer, which), device_id_type=MESH
            )

    toward(1, greet)
    pl.semaphore_signal(
        barrier, inc=1, device_id=(group, me, 1 - core), device_id_type=MESH
    )

    value_copies = [
        pltpu.make_async_copy(big_v, own_v, own_sem.at[0]),
        pltpu.make_async_copy(big_read, read_big, own_sem.at[1]),
        pltpu.make_async_copy(small_v, own_few_v, own_sem.at[2]),
        pltpu.make_async_copy(small_read, read_small, own_sem.at[3]),
    ]
    for copy in value_copies:
        copy.start()
    guide_copy = pltpu.make_async_copy(guidance, guide, own_sem.at[4])
    guide_copy.start()
    pltpu.make_async_copy(
        window(big_k, me, width), row_block(all_k, me, rows), big_recv.at[0]
    ).start()

    pltpu.make_async_copy(
        window(big_q, me, width), row_block(all_q, me, rows), big_recv.at[1 + behind]
    ).start()

    @pl.when(core == host)
    def _():
        for item in (0, 2):
            source, target = few_pairs[item]
            pltpu.make_async_copy(
                window(source, me, few_width),
                row_block(target, me * m + host, few_rows),
                few_recv.at[item + behind if item == 2 else item],
            ).start()

    for copy in value_copies:
        copy.wait()
    for seq in range(n):
        terms = []
        for head in range(heads_here):
            columns = slice(seq * width + head * DH, seq * width + (head + 1) * DH)
            terms.append(read_out(own_v[:, columns], read_big[:, columns]))
        ready_w[seq] = jnp.concatenate(terms, axis=1).astype(ready_w.dtype)
        columns = slice(seq * few_width, (seq + 1) * few_width)
        term = read_out(own_few_v[:, columns], read_small[:, columns])
        term = jnp.concatenate([term[: few_rows // 2], term[few_rows // 2 :]], axis=1)
        ready_few[seq] = term.astype(ready_few.dtype)

    def start_queries(peer):
        few_copy(2, peer).start()
        query_copy(peer).start()

    def start_early(peer):
        for item in (0, 1):
            few_copy(item, peer).start()
        key_copy(peer).start()
        value_copy(peer).start()
        pl.when(me == 0)(functools.partial(start_queries, peer))

    def start_late(peer):
        pl.when(me != 0)(functools.partial(start_queries, peer))

    def pass_on(index):
        def act(peer):
            pl.semaphore_signal(
                near.at[index], inc=1, device_id=(group, peer, core), device_id_type=MESH
            )

        return act

    pl.semaphore_wait(barrier, m * chips_at(1) + m - 1)
    toward(1, pass_on(0))
    toward(1, start_early, True)
    toward(1, start_early, False)
    known, index = 1, 0
    while known < rungs:
        pl.semaphore_wait(near.at[index], chips_at(known))
        reach = min(2 * known, rungs)
        index += 1
        if reach < rungs:
            toward(reach, pass_on(index))
        for distance in range(known + 1, reach + 1):
            toward(distance, start_early, True)
            toward(distance, start_early, False)
        held, known = known, reach
    for distance in range(held + 1, rungs + 1):
        toward(distance, start_late)
    for distance in range(held, 0, -1):
        toward(distance, start_late)

    @pl.when(core != host)
    def _():
        for item in range(3):
            few_copy(item, me).start()

    all_w[pl.ds(pl.multiple_of(me * rows, rows), rows), :] = ready_w[me]
    guide_copy.wait()
    weight_value = guide[0]

    def attend_rows(first, count, few_waits, query_waits):
        block = pl.ds(first, count)
        lanes = lax.broadcasted_iota(jnp.int32, (count, 2 * lat), 1)

        @pl.when(core == host)
        def _():
            few_waits()
            probs, totals = softmax_parts(few_q[block, :], few_k[...])
            pairs = few_w[...].astype(jnp.float32).reshape(n * m * few_rows // 2, 2 * lat)
            sides = [
                side.reshape(n * m, few_rows // 2, 2 * lat)
                for side in (pairs, pltpu.roll(pairs, lat, 1))
            ]
            held = jnp.concatenate(sides, axis=1).reshape(tokens, 2 * lat)
            term = jnp.dot(probs, held.astype(few_w.dtype), preferred_element_type=jnp.float32)
            small_part[block, :] = jnp.where(lanes < lat, weight_value * term / totals, 0.0)

        @pl.when(core != host)
        def _():
            small_part[block, :] = jnp.zeros((count, 2 * lat), jnp.float32)

        query_waits()
        held = all_w[...]
        parts = []
        for head in range(heads_here):
            columns = slice(head * DH, (head + 1) * DH)
            probs, totals = softmax_parts(all_q[block, columns], all_k[:, columns])
            parts.append((jnp.dot(probs, held, preferred_element_type=jnp.float32), totals))
        (left, left_totals), (right, right_totals) = parts
        totals = jnp.where(lanes < lat, left_totals, right_totals)
        term = (1.0 + weight_value) * (jnp.where(lanes < lat, left, right) / totals)
        term = term - small_part[block, :]
        latent[block, :] = term + pltpu.roll(term, lat, 1)
        pair_rows = count // 2
        even = latent[pl.ds(first, pair_rows, stride=2), :]
        odd = latent[pl.ds(first + 1, pair_rows, stride=2), :]
        return jnp.where(lanes[:pair_rows] < lat, even, odd)

    later = tokens - rows

    def first_few_waits():
        await_bytes(few_q.at[pl.ds(0, rows), :], few_recv.at[2])

    def later_few_waits():
        await_bytes(few_q.at[pl.ds(0, later), :], few_recv.at[3])

    def first_waits():
        await_bytes(all_q.at[pl.ds(0, rows), :], big_recv.at[1])

    def later_waits():
        await_bytes(all_q.at[pl.ds(0, later), :], big_recv.at[2])

    def attend_first():
        first_stage[...] = attend_rows(0, rows, first_few_waits, first_waits)

    @pl.when(core == host)
    def _():
        few_w[me * m + host] = ready_few[me]
        await_bytes(few_k, few_recv.at[0])
        await_bytes(few_w.at[pl.ds(0, n * m - 1)], few_recv.at[1])

    await_bytes(all_k, big_recv.at[0])
    await_bytes(all_w.at[pl.ds(0, later), :], value_sem.at[1])

    @pl.when(me != 0)
    def _():
        attend_first()
        for which in range(m):
            first_copy(which).start()

    stage[...] = attend_rows(rows, later, later_few_waits, later_waits).reshape(
        (n - 1) * m, part, 2 * lat
    )

    def start_back(peer):
        for which in range(m):
            back_copy(peer, which, stage.at[(peer - 1) * m + which]).start()

    for peer in range(1, n):
        pl.when(me != peer)(functools.partial(start_back, peer))

    @pl.when(me != 0)
    def _():
        own = (me - 1) * m
        arrived[me * m + core] = stage[own + core]
        back_copy(me, 1 - core, stage.at[own + 1 - core]).start()

    @pl.when(me == 0)
    def _():
        attend_first()
        first_arrived[core] = first_stage[...]
        first_copy(1 - core).start()

    @pl.when(me == 0)
    def _():
        await_bytes(first_arrived.at[pl.ds(0, n * m - 1)], first_sem.at[1])
        out[...] = jnp.sum(first_arrived[...], axis=0)
        await_bytes(stage, back_sem.at[0])
        await_bytes(first_stage, first_sem.at[0])

    @pl.when(me != 0)
    def _():
        await_bytes(arrived.at[pl.ds(0, n * m - 1)], back_sem.at[1])
        swap[0] = jnp.sum(arrived[...], axis=0)
        swap_copy().start()
        out[pl.ds(pl.multiple_of(core * part, part), part), :] = swap[0]
        await_bytes(arrived.at[pl.ds(0, n * m - 1 - m)], back_sem.at[0])
        await_bytes(first_arrived.at[pl.ds(0, m)], first_sem.at[0])

    await_bytes(all_k.at[pl.ds(0, later), :], big_send.at[0])
    await_bytes(all_q.at[pl.ds(0, later), :], big_send.at[1])
    await_bytes(all_w.at[pl.ds(0, later), :], value_sem.at[0])

    def await_few(chips):
        for item in (0, 2):
            await_bytes(few_pairs[item][1].at[pl.ds(0, chips * few_rows), :], few_send.at[item])
        await_bytes(few_w.at[pl.ds(0, chips)], few_send.at[1])

    pl.when(core == host)(functools.partial(await_few, n - 1))
    pl.when(core != host)(functools.partial(await_few, n))

    @pl.when(me != 0)
    def _():
        swap_copy().wait()
        out[pl.ds(pl.multiple_of((1 - core) * part, part), part), :] = swap[1]


def fused(
    n,
    m,
    big_queries,
    big_keys,
    big_values,
    small_queries,
    small_keys,
    small_values,
    big_readout,
    small_readout,
    guidance,
):
    rows, columns = big_queries.shape
    few_rows, few_columns = small_queries.shape
    width, few_width = columns // n, few_columns // n
    tokens = rows * n
    lat = big_readout.shape[1]
    half = rows // 2
    part = half // m
    kind = jnp.bfloat16
    dma = pltpu.SemaphoreType.DMA
    return pl.pallas_call(
        functools.partial(window_kernel, n, m),
        out_shape=pltpu.VMEM((half, 2 * lat), jnp.float32),
        in_specs=[pl.BlockSpec(memory_space=pl.ANY)] * 9,
        out_specs=pl.BlockSpec(memory_space=pltpu.VMEM),
        scratch_shapes=[
            pltpu.VMEM((tokens, width), kind),
            pltpu.VMEM((tokens, width), kind),
            pltpu.VMEM((tokens, 2 * lat), kind),
            pltpu.VMEM((tokens, few_width), kind),
            pltpu.VMEM((tokens, few_width), kind),
            pltpu.VMEM((n * m, few_rows // 2, 2 * lat), kind),
            pltpu.VMEM((rows, columns), kind),
            pltpu.VMEM((few_rows, few_columns), kind),
            pltpu.VMEM((lat, columns), kind),
            pltpu.VMEM((lat, few_columns), kind),
            pltpu.VMEM((n, rows, 2 * lat), kind),
            pltpu.VMEM((n, few_rows // 2, 2 * lat), kind),
            pltpu.VMEM((tokens, 2 * lat), jnp.float32),
            pltpu.VMEM((tokens, 2 * lat), jnp.float32),
            pltpu.VMEM((half, 2 * lat), jnp.float32),
            pltpu.VMEM(((n - 1) * m, part, 2 * lat), jnp.float32),
            pltpu.VMEM((n * m, half, 2 * lat), jnp.float32),
            pltpu.VMEM((n * m, part, 2 * lat), jnp.float32),
            pltpu.VMEM((2, part, 2 * lat), jnp.float32),
            pltpu.SMEM((1,), jnp.float32),
            pltpu.SemaphoreType.REGULAR(((n // 2 - 1).bit_length(),)),
            dma((5,)),
            dma((2,)),
            dma((3,)),
            dma((2,)),
            dma((3,)),
            dma((4,)),
            dma((2,)),
            dma((2,)),
            dma((2,)),
        ],
        compiler_params=pltpu.CompilerParams(collective_id=0, has_side_effects=True),
        name="fused_window",
    )(
        guidance,
        big_queries,
        big_keys,
        big_values,
        small_queries,
        small_keys,
        small_values,
        big_readout.T,
        small_readout.T,
    )


def fits(n, m, big_queries, small_queries, lat):
    rows, columns = big_queries.shape
    few_rows, few_columns = small_queries.shape
    return (
        n > 2
        and n % 2 == 0
        and m == 2
        and n * rows <= 512
        and columns == 2 * n * DH
        and few_columns == n * DH
        and rows == m * few_rows
        and few_rows % 16 == 0
        and 2 * lat == 128
    )


def shards(*arguments):
    n, m = lax.axis_size("seq"), lax.axis_size("head")
    if fits(n, m, arguments[0], arguments[3], arguments[6].shape[1]):
        return fused(n, m, *arguments)
    return exchanged(*arguments)


def solution(mesh):
    placed = (
        P(("groups", "seq"), "head"),
        P(("groups", "seq"), "head"),
        P(("groups", "seq"), "head"),
        P(("groups", "seq", "head"), None),
        P(("groups", "seq", "head"), None),
        P(("groups", "seq", "head"), None),
        P("head", None),
        P(),
        P("groups"),
    )
    return jax.shard_map(
        shards, mesh=mesh, in_specs=placed, out_specs=P(("groups", "seq"), None), check_vma=False
    )
```

```python
import functools
import math

import jax
import jax.numpy as jnp
from jax import lax
from jax.experimental import pallas as pl
from jax.experimental.pallas import tpu as pltpu
from jax.sharding import PartitionSpec as P

DH = 128


def split_heads(matrix, blocks, parts):
    rows_here, columns = matrix.shape
    shaped = matrix.reshape(blocks, rows_here // blocks, parts, columns // parts)
    shaped = jnp.transpose(shaped, (0, 2, 1, 3))
    return shaped.reshape(blocks * parts, rows_here // blocks, columns // parts)


def copy_heads(matrix, blocks, parts):
    rows_here, columns = matrix.shape
    shaped = jnp.transpose(matrix.reshape(rows_here, parts, columns // parts), (1, 0, 2))
    shaped = jnp.broadcast_to(shaped[None], (blocks, parts, rows_here, columns // parts))
    return shaped.reshape(blocks * parts, rows_here, columns // parts)


def join_heads(stacked, blocks, parts):
    pieces, rows_here, columns = stacked.shape
    shaped = stacked.reshape(blocks, parts, rows_here, columns)
    shaped = jnp.transpose(shaped, (0, 2, 1, 3))
    return shaped.reshape(blocks * rows_here, parts * columns)


def attend(query_rows, key_rows, value_rows):
    query_count = query_rows.shape[0]
    heads_here = query_rows.shape[1] // DH
    key_count = key_rows.shape[0]
    block_height = math.gcd(query_count, 256)
    block_count = query_count // block_height
    query_blocks = query_rows.reshape(block_count, block_height, heads_here, DH)
    key_split = key_rows.reshape(key_count, heads_here, DH)
    value_split = value_rows.reshape(key_count, heads_here, DH)
    score_scale = 1.0 / math.sqrt(DH)

    def one_block(query_block):
        scores = (
            jnp.einsum("qgd,kgd->gqk", query_block, key_split, preferred_element_type=jnp.float32)
            * score_scale
        )
        row_max = jnp.max(scores, axis=2, keepdims=True)
        probs = jnp.exp(scores - row_max)
        totals = jnp.sum(probs, axis=2, keepdims=True)
        weights = probs.astype(jnp.bfloat16)
        accumulated = jnp.einsum(
            "gqk,kgd->gqd", weights, value_split, preferred_element_type=jnp.float32
        )
        attended = accumulated / totals
        attended = jnp.transpose(attended, (1, 0, 2)).reshape(block_height, heads_here * DH)
        return attended.astype(jnp.bfloat16)

    outputs = lax.map(one_block, query_blocks)
    return outputs.reshape(query_count, heads_here * DH)


def exchanged(
    big_queries,
    big_keys,
    big_values,
    small_queries,
    small_keys,
    small_values,
    big_readout,
    small_readout,
    guidance,
):
    seq_count = lax.axis_size("seq")
    big_heads = big_queries.shape[1] // DH
    big_group = max(big_heads // seq_count, 1)
    big_blocks = max(seq_count // big_heads, 1)
    big_parts = big_heads // big_group
    query_rows = lax.all_to_all(
        split_heads(big_queries, big_blocks, big_parts),
        "seq",
        split_axis=0,
        concat_axis=1,
        tiled=True,
    )[0]
    key_copies, value_copies = (
        lax.all_to_all(
            copy_heads(big_keys, big_blocks, big_parts),
            "seq",
            split_axis=0,
            concat_axis=1,
            tiled=True,
        ),
        lax.all_to_all(
            copy_heads(big_values, big_blocks, big_parts),
            "seq",
            split_axis=0,
            concat_axis=1,
            tiled=True,
        ),
    )
    key_rows = key_copies[0]
    value_rows = value_copies[0]
    big_out = attend(query_rows, key_rows, value_rows)
    big_back = lax.all_to_all(big_out[None], "seq", split_axis=1, concat_axis=0, tiled=True)
    big_attention = join_heads(big_back, big_blocks, big_parts)
    big_partial = jnp.dot(big_attention, big_readout, preferred_element_type=jnp.float32)
    small_heads = small_queries.shape[1] // DH
    small_group = max(small_heads // seq_count, 1)
    small_blocks = max(seq_count // small_heads, 1)
    small_parts = small_heads // small_group
    small_query_rows = lax.all_to_all(
        split_heads(small_queries, small_blocks, small_parts),
        "seq",
        split_axis=0,
        concat_axis=1,
        tiled=True,
    )[0]
    key_copies, value_copies = (
        lax.all_to_all(
            copy_heads(small_keys, small_blocks, small_parts),
            "seq",
            split_axis=0,
            concat_axis=1,
            tiled=True,
        ),
        lax.all_to_all(
            copy_heads(small_values, small_blocks, small_parts),
            "seq",
            split_axis=0,
            concat_axis=1,
            tiled=True,
        ),
    )
    small_key_rows, small_value_rows = (
        lax.all_gather(key_copies[0], "head", axis=0, tiled=True),
        lax.all_gather(value_copies[0], "head", axis=0, tiled=True),
    )
    small_out = attend(small_query_rows, small_key_rows, small_value_rows)
    small_back = lax.all_to_all(small_out[None], "seq", split_axis=1, concat_axis=0, tiled=True)
    small_attention = join_heads(small_back, small_blocks, small_parts)
    small_latent = jnp.dot(small_attention, small_readout, preferred_element_type=jnp.float32)
    weight_value = guidance[0]
    core_index = lax.axis_index("head")
    placed = lax.dynamic_update_slice(
        jnp.zeros_like(big_partial),
        small_latent,
        (core_index * small_latent.shape[0], jnp.zeros((), jnp.int32)),
    )
    blended = lax.psum((1.0 + weight_value) * big_partial - weight_value * placed, "head")
    return blended.reshape(blended.shape[0] // 2, 2 * blended.shape[1])


MESH = pl.DeviceIdType.MESH


def softmax_parts(query_head, key_head):
    scores = lax.dot_general(
        query_head, key_head, (((1,), (1,)), ((), ())), preferred_element_type=jnp.float32
    ) * (1.0 / math.sqrt(DH))
    row_max = jnp.max(scores, axis=1, keepdims=True)
    probs = jnp.exp(scores - row_max)
    totals = jnp.sum(probs, axis=1, keepdims=True)
    return probs.astype(jnp.bfloat16), totals


def read_out(values, readout):
    return lax.dot_general(
        values, readout, (((1,), (1,)), ((), ())), preferred_element_type=jnp.float32
    )


def window_kernel(
    n,
    m,
    guidance,
    big_q,
    big_k,
    big_v,
    small_q,
    small_k,
    small_v,
    big_read,
    small_read,
    out,
    all_q,
    all_k,
    all_w,
    few_q,
    few_k,
    few_w,
    own_v,
    own_few_v,
    read_big,
    read_small,
    ready_w,
    ready_few,
    small_part,
    latent,
    first_stage,
    stage,
    first_arrived,
    arrived,
    swap,
    guide,
    near,
    own_sem,
    big_send,
    big_recv,
    value_sem,
    few_send,
    few_recv,
    first_sem,
    back_sem,
    swap_sem,
):
    group = lax.axis_index("groups")
    me = lax.axis_index("seq")
    core = lax.axis_index("head")
    host = m - 1
    rungs = n // 2
    rung, side = lax.div(me, 2), lax.rem(me, 2)
    rows = big_q.shape[0]
    tokens = n * rows
    width = all_q.shape[1]
    few_rows = small_q.shape[0]
    few_width = few_q.shape[1]
    heads_here = width // DH
    lat = big_read.shape[0]
    half = rows // 2
    part = half // m

    def window(ref, index, size):
        return ref.at[:, pl.ds(pl.multiple_of(index * size, size), size)]

    def row_block(ref, index, size):
        return ref.at[pl.ds(pl.multiple_of(index * size, size), size), :]

    def toward(distance, act, crossing=None):
        for up in sorted(range(1 - rungs, rungs), key=lambda up: -abs(up)):
            if distance - abs(up) not in (0, 1):
                continue
            there = rung + up
            wanted = (there >= 0) & (there < rungs)
            if crossing is not None:
                other = (rung < rungs // 2) != (there < rungs // 2)
                wanted = wanted & (other if crossing else jnp.logical_not(other))
            peer = there * 2 + lax.rem(side + distance - abs(up), 2)
            pl.when(wanted)(functools.partial(act, peer))

    def chips_at(distance):
        count = 0
        for up in range(1 - rungs, rungs):
            if distance - abs(up) in (0, 1):
                there = rung + up
                count = count + ((there >= 0) & (there < rungs)).astype(jnp.int32)
        return count

    behind = (me != 0).astype(jnp.int32)
    few_pairs = ((small_k, few_k), (ready_few, few_w), (small_q, few_q))

    def key_copy(peer):
        return pltpu.make_async_remote_copy(
            src_ref=window(big_k, peer, width),
            dst_ref=row_block(all_k, me, rows),
            send_sem=big_send.at[0],
            recv_sem=big_recv.at[0],
            device_id=(group, peer, core),
            device_id_type=MESH,
        )

    def query_copy(peer):
        return pltpu.make_async_remote_copy(
            src_ref=window(big_q, peer, width),
            dst_ref=row_block(all_q, me, rows),
            send_sem=big_send.at[1],
            recv_sem=big_recv.at[1 + behind],
            device_id=(group, peer, core),
            device_id_type=MESH,
        )

    def value_copy(peer):
        return pltpu.make_async_remote_copy(
            src_ref=ready_w.at[peer],
            dst_ref=row_block(all_w, me, rows),
            send_sem=value_sem.at[0],
            recv_sem=value_sem.at[1],
            device_id=(group, peer, core),
            device_id_type=MESH,
        )

    def few_copy(item, peer):
        source, target = few_pairs[item]
        return pltpu.make_async_remote_copy(
            src_ref=source.at[peer] if item == 1 else window(source, peer, few_width),
            dst_ref=(
                target.at[me * m + core]
                if item == 1
                else row_block(target, me * m + core, few_rows)
            ),
            send_sem=few_send.at[item],
            recv_sem=few_recv.at[item + behind if item == 2 else item],
            device_id=(group, peer, host),
            device_id_type=MESH,
        )

    def back_copy(peer, which, source):
        return pltpu.make_async_remote_copy(
            src_ref=source,
            dst_ref=arrived.at[me * m + core],
            send_sem=back_sem.at[0],
            recv_sem=back_sem.at[1],
            device_id=(group, peer, which),
            device_id_type=MESH,
        )

    def first_copy(which):
        return pltpu.make_async_remote_copy(
            src_ref=first_stage,
            dst_ref=first_arrived.at[me * m + core],
            send_sem=first_sem.at[0],
            recv_sem=first_sem.at[1],
            device_id=(group, 0, which),
            device_id_type=MESH,
        )

    def swap_copy():
        return pltpu.make_async_remote_copy(
            src_ref=swap.at[0],
            dst_ref=swap.at[1],
            send_sem=swap_sem.at[0],
            recv_sem=swap_sem.at[1],
            device_id=(group, me, 1 - core),
            device_id_type=MESH,
        )

    def await_bytes(ref, sem):
        pltpu.make_async_copy(ref, ref, sem).wait()

    barrier = pltpu.get_barrier_semaphore()

    def greet(peer):
        for which in range(m):
            pl.semaphore_signal(
                barrier, inc=1, device_id=(group, peer, which), device_id_type=MESH
            )

    toward(1, greet)
    pl.semaphore_signal(
        barrier, inc=1, device_id=(group, me, 1 - core), device_id_type=MESH
    )

    value_copies = [
        pltpu.make_async_copy(big_v, own_v, own_sem.at[0]),
        pltpu.make_async_copy(big_read, read_big, own_sem.at[1]),
        pltpu.make_async_copy(small_v, own_few_v, own_sem.at[2]),
        pltpu.make_async_copy(small_read, read_small, own_sem.at[3]),
    ]
    for copy in value_copies:
        copy.start()
    guide_copy = pltpu.make_async_copy(guidance, guide, own_sem.at[4])
    guide_copy.start()
    pltpu.make_async_copy(
        window(big_k, me, width), row_block(all_k, me, rows), big_recv.at[0]
    ).start()

    pltpu.make_async_copy(
        window(big_q, me, width), row_block(all_q, me, rows), big_recv.at[1 + behind]
    ).start()

    @pl.when(core == host)
    def _():
        for item in (0, 2):
            source, target = few_pairs[item]
            pltpu.make_async_copy(
                window(source, me, few_width),
                row_block(target, me * m + host, few_rows),
                few_recv.at[item + behind if item == 2 else item],
            ).start()

    for copy in value_copies:
        copy.wait()
    for seq in range(n):
        terms = []
        for head in range(heads_here):
            columns = slice(seq * width + head * DH, seq * width + (head + 1) * DH)
            terms.append(read_out(own_v[:, columns], read_big[:, columns]))
        ready_w[seq] = jnp.concatenate(terms, axis=1).astype(ready_w.dtype)
        columns = slice(seq * few_width, (seq + 1) * few_width)
        term = read_out(own_few_v[:, columns], read_small[:, columns])
        term = jnp.concatenate([term[: few_rows // 2], term[few_rows // 2 :]], axis=1)
        ready_few[seq] = term.astype(ready_few.dtype)

    def start_queries(peer):
        few_copy(2, peer).start()
        query_copy(peer).start()

    def start_early(peer):
        for item in (0, 1):
            few_copy(item, peer).start()
        key_copy(peer).start()
        value_copy(peer).start()
        pl.when(me == 0)(functools.partial(start_queries, peer))

    def start_late(peer):
        pl.when(me != 0)(functools.partial(start_queries, peer))

    def pass_on(index):
        def act(peer):
            pl.semaphore_signal(
                near.at[index], inc=1, device_id=(group, peer, core), device_id_type=MESH
            )

        return act

    pl.semaphore_wait(barrier, m * chips_at(1) + m - 1)
    toward(1, pass_on(0))
    toward(1, start_early, True)
    toward(1, start_early, False)
    known, index = 1, 0
    while known < rungs:
        pl.semaphore_wait(near.at[index], chips_at(known))
        reach = min(2 * known, rungs)
        index += 1
        if reach < rungs:
            toward(reach, pass_on(index))
        for distance in range(known + 1, reach + 1):
            toward(distance, start_early, True)
            toward(distance, start_early, False)
        held, known = known, reach
    for peer in range(n - 1, -1, -1):
        pl.when(me != peer)(functools.partial(start_late, peer))

    @pl.when(core != host)
    def _():
        for item in range(3):
            few_copy(item, me).start()

    all_w[pl.ds(pl.multiple_of(me * rows, rows), rows), :] = ready_w[me]
    guide_copy.wait()
    weight_value = guide[0]

    def attend_rows(first, count, few_waits, query_waits):
        block = pl.ds(first, count)
        lanes = lax.broadcasted_iota(jnp.int32, (count, 2 * lat), 1)

        @pl.when(core == host)
        def _():
            few_waits()
            probs, totals = softmax_parts(few_q[block, :], few_k[...])
            pairs = few_w[...].astype(jnp.float32).reshape(n * m * few_rows // 2, 2 * lat)
            sides = [
                side.reshape(n * m, few_rows // 2, 2 * lat)
                for side in (pairs, pltpu.roll(pairs, lat, 1))
            ]
            held = jnp.concatenate(sides, axis=1).reshape(tokens, 2 * lat)
            term = jnp.dot(probs, held.astype(few_w.dtype), preferred_element_type=jnp.float32)
            small_part[block, :] = jnp.where(lanes < lat, weight_value * term / totals, 0.0)

        @pl.when(core != host)
        def _():
            small_part[block, :] = jnp.zeros((count, 2 * lat), jnp.float32)

        query_waits()
        held = all_w[...]
        parts = []
        for head in range(heads_here):
            columns = slice(head * DH, (head + 1) * DH)
            probs, totals = softmax_parts(all_q[block, columns], all_k[:, columns])
            parts.append((jnp.dot(probs, held, preferred_element_type=jnp.float32), totals))
        (left, left_totals), (right, right_totals) = parts
        totals = jnp.where(lanes < lat, left_totals, right_totals)
        term = (1.0 + weight_value) * (jnp.where(lanes < lat, left, right) / totals)
        term = term - small_part[block, :]
        latent[block, :] = term + pltpu.roll(term, lat, 1)
        pair_rows = count // 2
        even = latent[pl.ds(first, pair_rows, stride=2), :]
        odd = latent[pl.ds(first + 1, pair_rows, stride=2), :]
        return jnp.where(lanes[:pair_rows] < lat, even, odd)

    later = tokens - rows

    def first_few_waits():
        await_bytes(few_q.at[pl.ds(0, rows), :], few_recv.at[2])

    def later_few_waits():
        await_bytes(few_q.at[pl.ds(0, later), :], few_recv.at[3])

    def first_waits():
        await_bytes(all_q.at[pl.ds(0, rows), :], big_recv.at[1])

    def later_waits():
        await_bytes(all_q.at[pl.ds(0, later), :], big_recv.at[2])

    def attend_first():
        first_stage[...] = attend_rows(0, rows, first_few_waits, first_waits)

    @pl.when(core == host)
    def _():
        few_w[me * m + host] = ready_few[me]
        await_bytes(few_k, few_recv.at[0])
        await_bytes(few_w.at[pl.ds(0, n * m - 1)], few_recv.at[1])

    await_bytes(all_k, big_recv.at[0])
    await_bytes(all_w.at[pl.ds(0, later), :], value_sem.at[1])

    @pl.when(me != 0)
    def _():
        attend_first()
        for which in range(m):
            first_copy(which).start()

    stage[...] = attend_rows(rows, later, later_few_waits, later_waits).reshape(
        (n - 1) * m, part, 2 * lat
    )

    def start_back(peer):
        for which in range(m):
            back_copy(peer, which, stage.at[(peer - 1) * m + which]).start()

    for peer in range(1, n):
        pl.when(me != peer)(functools.partial(start_back, peer))

    @pl.when(me != 0)
    def _():
        own = (me - 1) * m
        arrived[me * m + core] = stage[own + core]
        back_copy(me, 1 - core, stage.at[own + 1 - core]).start()

    @pl.when(me == 0)
    def _():
        attend_first()
        first_arrived[core] = first_stage[...]
        first_copy(1 - core).start()

    @pl.when(me == 0)
    def _():
        await_bytes(first_arrived.at[pl.ds(0, n * m - 1)], first_sem.at[1])
        out[...] = jnp.sum(first_arrived[...], axis=0)
        await_bytes(stage, back_sem.at[0])
        await_bytes(first_stage, first_sem.at[0])

    @pl.when(me != 0)
    def _():
        await_bytes(arrived.at[pl.ds(0, n * m - 1)], back_sem.at[1])
        swap[0] = jnp.sum(arrived[...], axis=0)
        swap_copy().start()
        out[pl.ds(pl.multiple_of(core * part, part), part), :] = swap[0]
        await_bytes(arrived.at[pl.ds(0, n * m - 1 - m)], back_sem.at[0])
        await_bytes(first_arrived.at[pl.ds(0, m)], first_sem.at[0])

    await_bytes(all_k.at[pl.ds(0, later), :], big_send.at[0])
    await_bytes(all_q.at[pl.ds(0, later), :], big_send.at[1])
    await_bytes(all_w.at[pl.ds(0, later), :], value_sem.at[0])

    def await_few(chips):
        for item in (0, 2):
            await_bytes(few_pairs[item][1].at[pl.ds(0, chips * few_rows), :], few_send.at[item])
        await_bytes(few_w.at[pl.ds(0, chips)], few_send.at[1])

    pl.when(core == host)(functools.partial(await_few, n - 1))
    pl.when(core != host)(functools.partial(await_few, n))

    @pl.when(me != 0)
    def _():
        swap_copy().wait()
        out[pl.ds(pl.multiple_of((1 - core) * part, part), part), :] = swap[1]


def fused(
    n,
    m,
    big_queries,
    big_keys,
    big_values,
    small_queries,
    small_keys,
    small_values,
    big_readout,
    small_readout,
    guidance,
):
    rows, columns = big_queries.shape
    few_rows, few_columns = small_queries.shape
    width, few_width = columns // n, few_columns // n
    tokens = rows * n
    lat = big_readout.shape[1]
    half = rows // 2
    part = half // m
    kind = jnp.bfloat16
    dma = pltpu.SemaphoreType.DMA
    return pl.pallas_call(
        functools.partial(window_kernel, n, m),
        out_shape=pltpu.VMEM((half, 2 * lat), jnp.float32),
        in_specs=[pl.BlockSpec(memory_space=pl.ANY)] * 9,
        out_specs=pl.BlockSpec(memory_space=pltpu.VMEM),
        scratch_shapes=[
            pltpu.VMEM((tokens, width), kind),
            pltpu.VMEM((tokens, width), kind),
            pltpu.VMEM((tokens, 2 * lat), kind),
            pltpu.VMEM((tokens, few_width), kind),
            pltpu.VMEM((tokens, few_width), kind),
            pltpu.VMEM((n * m, few_rows // 2, 2 * lat), kind),
            pltpu.VMEM((rows, columns), kind),
            pltpu.VMEM((few_rows, few_columns), kind),
            pltpu.VMEM((lat, columns), kind),
            pltpu.VMEM((lat, few_columns), kind),
            pltpu.VMEM((n, rows, 2 * lat), kind),
            pltpu.VMEM((n, few_rows // 2, 2 * lat), kind),
            pltpu.VMEM((tokens, 2 * lat), jnp.float32),
            pltpu.VMEM((tokens, 2 * lat), jnp.float32),
            pltpu.VMEM((half, 2 * lat), jnp.float32),
            pltpu.VMEM(((n - 1) * m, part, 2 * lat), jnp.float32),
            pltpu.VMEM((n * m, half, 2 * lat), jnp.float32),
            pltpu.VMEM((n * m, part, 2 * lat), jnp.float32),
            pltpu.VMEM((2, part, 2 * lat), jnp.float32),
            pltpu.SMEM((1,), jnp.float32),
            pltpu.SemaphoreType.REGULAR(((n // 2 - 1).bit_length(),)),
            dma((5,)),
            dma((2,)),
            dma((3,)),
            dma((2,)),
            dma((3,)),
            dma((4,)),
            dma((2,)),
            dma((2,)),
            dma((2,)),
        ],
        compiler_params=pltpu.CompilerParams(collective_id=0, has_side_effects=True),
        name="fused_window",
    )(
        guidance,
        big_queries,
        big_keys,
        big_values,
        small_queries,
        small_keys,
        small_values,
        big_readout.T,
        small_readout.T,
    )


def fits(n, m, big_queries, small_queries, lat):
    rows, columns = big_queries.shape
    few_rows, few_columns = small_queries.shape
    return (
        n > 2
        and n % 2 == 0
        and m == 2
        and n * rows <= 512
        and columns == 2 * n * DH
        and few_columns == n * DH
        and rows == m * few_rows
        and few_rows % 16 == 0
        and 2 * lat == 128
    )


def shards(*arguments):
    n, m = lax.axis_size("seq"), lax.axis_size("head")
    if fits(n, m, arguments[0], arguments[3], arguments[6].shape[1]):
        return fused(n, m, *arguments)
    return exchanged(*arguments)


def solution(mesh):
    placed = (
        P(("groups", "seq"), "head"),
        P(("groups", "seq"), "head"),
        P(("groups", "seq"), "head"),
        P(("groups", "seq", "head"), None),
        P(("groups", "seq", "head"), None),
        P(("groups", "seq", "head"), None),
        P("head", None),
        P(),
        P("groups"),
    )
    return jax.shard_map(
        shards, mesh=mesh, in_specs=placed, out_specs=P(("groups", "seq"), None), check_vma=False
    )
```
